32 devices in a mesh: grp: 2 (over y), seq: 16 (over z, x, core).
Axes of the slice: x: 2, y: 2, z: 4, core: 2. Of those that a mesh axis runs over, the one named last changes fastest.
Arguments:
- queries: bfloat16 [4096, 128], P(('grp', 'seq')), parts along dimension 0, may hold values from -6 to 6
- keys: bfloat16 [4096, 128], P(('grp', 'seq')), parts along dimension 0, may hold values from -6 to 6
- values: bfloat16 [4096, 128], P(('grp', 'seq')), parts along dimension 0, may hold values from -6 to 6
- log_gate: float32 [4096], P(('grp', 'seq')), parts along dimension 0, may hold values from -1 to 0, as said below
- out_grad: bfloat16 [4096, 128], P(('grp', 'seq')), parts along dimension 0, may hold values from -6 to 6
- segment_order: int32 [64], P(('grp', 'seq')), parts along dimension 0, may hold values from 0 to 31, each once
Outputs:
- attn_out: bfloat16 [4096, 128], P(('grp', 'seq')), parts along dimension 0
- query_grad: float32 [4096, 128], P(('grp', 'seq')), parts along dimension 0
- key_grad: float32 [4096, 128], P(('grp', 'seq')), parts along dimension 0
- value_grad: float32 [4096, 128], P(('grp', 'seq')), parts along dimension 0
- gate_grad: float32 [4096], P(('grp', 'seq')), parts along dimension 0
The draws below stay inside these ranges and needn't reach their ends.
There are 2 independent parts, one for each index of `grp`. The reference program is written for one: setup_inputs(seed, part) draws one part's arguments, and reference() takes and returns one part's arrays. A program takes and returns all parts, laid end to end along the dimension named above; each array names one. Nothing has to cross between parts.
Inputs may be any that keep to these rules, and one draw needn't show every extreme that they name: `log_gate`: every gate is below one. `segment_order`: each segment index appears once.
All inputs are finite; a program needn't handle non-finite values.
Results may differ from the reference program's by a relative error of at most 0.0095.
Values may be sent and summed in bfloat16 or wider, within the bound.
No kernel may reach another device: no remote copies, remote signals or barrier semaphores. Data moves between devices by JAX's collectives and lax.ppermute only.
A program may use at most 64 MiB of HBM per device.

```python
import jax
import jax.numpy as jnp
from jax import lax

DH = 128
PIECE_LENGTH = 64
SEGMENTS = 32
STREAM_LENGTH = 2048


def paired_rows(key):
    key_one, key_two = jax.random.split(jax.random.fold_in(key, 7), 2)
    query_rows = jnp.clip(1.6 * jax.random.normal(key_one, (STREAM_LENGTH, DH), jnp.float32), -6.0, 6.0)
    key_rows = jnp.clip(1.6 * jax.random.normal(key_two, (STREAM_LENGTH, DH), jnp.float32), -6.0, 6.0)
    return (query_rows, key_rows)


def draw_queries(key, part):
    return paired_rows(key)[0].astype(jnp.bfloat16)


def draw_keys(key, part):
    return paired_rows(key)[1].astype(jnp.bfloat16)


def draw_log_gate(key, part):
    base_key, factor_key, jump_place_seed, jump_size_seed = jax.random.split(jax.random.fold_in(key, 11), 4)
    lowest = 0.1 / STREAM_LENGTH
    highest = 2.0 / STREAM_LENGTH
    baseline_decay_level = jnp.exp(jax.random.uniform(base_key, (STREAM_LENGTH,), jnp.float32, jnp.log(lowest), jnp.log(highest)))
    forget_multiplier = jnp.exp(jax.random.uniform(factor_key, (STREAM_LENGTH // PIECE_LENGTH, 1), jnp.float32, jnp.log(0.4), jnp.log(2.5)))
    jump_positions_list = jax.random.randint(jump_place_seed, (3,), 0, STREAM_LENGTH)
    jump_sizes = jax.random.uniform(jump_size_seed, (3,), jnp.float32, 0.2, 0.5)
    jump_count = jnp.zeros((STREAM_LENGTH,), jnp.float32).at[jump_positions_list].add(jump_sizes)
    return -((baseline_decay_level.reshape(-1, PIECE_LENGTH) * forget_multiplier).reshape(-1) + jump_count)


def levels(stream_key, extent, cuts, low, top_value):
    level = 1.0
    for position, parts in cuts:
        steps = jax.random.uniform(jax.random.fold_in(jax.random.fold_in(stream_key, 6), position), (parts,), jnp.float32, low / len(cuts), top_value / len(cuts))
        level = level * jnp.repeat(jnp.exp(steps), extent[position] // parts).reshape((-1,) + (1,) * (len(extent) - 1 - position))
    return level


def scatter_about(key, extent, spread, bound, pieces=(), kind=jnp.bfloat16):
    result = jax.random.normal(key, extent, jnp.float32) * spread
    if len(pieces) > 0:
        result = levels(key, extent, pieces, -0.22, 0.18) * result
    return jnp.clip(result, min=-bound, max=bound).astype(kind)


def setup_inputs(seed: int = 0, part: int = 0) -> dict:
    key_of = jax.random.split(jax.random.key(seed), 7)
    part_splits = jax.random.split(jax.random.fold_in(key_of[6], part), 7)
    return {
        "queries": draw_queries(jax.random.fold_in(jax.random.fold_in(key_of[6], part), 71), part),
        "keys": draw_keys(jax.random.fold_in(jax.random.fold_in(key_of[6], part), 71), part),
        "values": scatter_about(part_splits[2], (STREAM_LENGTH, DH), 1.0, 6.0, ((0, 16),)),
        "log_gate": draw_log_gate(jax.random.fold_in(jax.random.fold_in(key_of[6], part), 71), part),
        "out_grad": scatter_about(part_splits[4], (STREAM_LENGTH, DH), 1.0, 6.0, ((0, 16),)),
        "segment_order": jax.random.permutation(part_splits[5], SEGMENTS).astype(jnp.int32),
    }


masked_value = -1e30


def reference(queries, keys, values, log_gate, out_grad, segment_order):
    total_len, width = queries.shape
    segment_rows = total_len // segment_order.shape[0]
    score_scale = width ** -0.5
    true_order = jnp.argsort(segment_order).astype(jnp.int32)
    offsets_in = jnp.arange(segment_rows, dtype=jnp.int32)
    positions = (segment_order[:, None] * segment_rows + offsets_in[None, :]).reshape(-1)
    ordered = log_gate.reshape(-1, segment_rows)[true_order].reshape(-1)
    gate_cum = jnp.cumsum(ordered).reshape(-1, segment_rows)[segment_order].reshape(-1)
    block = 1024 if total_len % 1024 == 0 else total_len
    count = total_len // block

    def block_scores(block_index):
        start = (block_index * block).astype(jnp.int32)
        rows = lax.dynamic_slice_in_dim(queries, start, block)
        row_gate = lax.dynamic_slice_in_dim(gate_cum, start, block)
        row_pos = lax.dynamic_slice_in_dim(positions, start, block)
        scores = jnp.dot(rows, keys.T, preferred_element_type=jnp.float32) * score_scale
        scores = scores + row_gate[:, None] - gate_cum[None, :]
        visible = positions[None, :] <= row_pos[:, None]
        return rows, jnp.where(visible, scores, masked_value)

    def forward_block(block_index):
        rows, kept = block_scores(block_index)
        top = jnp.max(kept, axis=1)
        log_total = top + jnp.log(jnp.sum(jnp.exp(kept - top[:, None]), axis=1))
        probs = jnp.exp(kept - log_total[:, None]).astype(jnp.bfloat16)
        return jnp.dot(probs, values, preferred_element_type=jnp.float32), log_total

    indices = jnp.arange(count, dtype=jnp.int32)
    out_blocks, total_blocks = lax.map(forward_block, indices)
    out_full = out_blocks.reshape(total_len, width)
    log_total = total_blocks.reshape(-1)
    attn_out = out_full.astype(jnp.bfloat16)
    row_delta = jnp.sum(out_grad.astype(jnp.float32) * out_full, axis=1)

    def backward_block(carry, block_index):
        key_acc, value_acc, column_acc = carry
        start = (block_index * block).astype(jnp.int32)
        rows, kept = block_scores(block_index)
        grad_rows = lax.dynamic_slice_in_dim(out_grad, start, block)
        row_total = lax.dynamic_slice_in_dim(log_total, start, block)
        delta_rows = lax.dynamic_slice_in_dim(row_delta, start, block)
        probs = jnp.exp(kept - row_total[:, None])
        dprob = jnp.dot(grad_rows, values.T, preferred_element_type=jnp.float32)
        dscore = probs * (dprob - delta_rows[:, None])
        low = dscore.astype(jnp.bfloat16)
        query_rows_grad = jnp.dot(low, keys, preferred_element_type=jnp.float32) * score_scale
        key_acc = key_acc + jnp.dot(low.T, rows, preferred_element_type=jnp.float32) * score_scale
        value_acc = value_acc + jnp.dot(probs.astype(jnp.bfloat16).T, grad_rows, preferred_element_type=jnp.float32)
        column_acc = column_acc + jnp.sum(dscore, axis=0)
        return (key_acc, value_acc, column_acc), query_rows_grad

    zeros_rows = jnp.zeros((total_len, width), jnp.float32)
    carry_init = (zeros_rows, zeros_rows, jnp.zeros((total_len,), jnp.float32))
    (key_grad, value_grad, column_acc), query_blocks = lax.scan(backward_block, carry_init, indices)
    query_grad = query_blocks.reshape(total_len, width)
    gate_point = -column_acc
    ordered_point = gate_point.reshape(-1, segment_rows)[true_order].reshape(-1)
    suffix = jnp.flip(jnp.cumsum(jnp.flip(ordered_point)))
    gate_grad = suffix.reshape(-1, segment_rows)[segment_order].reshape(-1)
    return attn_out, query_grad, key_grad, value_grad, gate_grad
```

```python
import jax
import jax.numpy as jnp
from jax import lax
from jax.experimental import pallas as pl
from jax.experimental.pallas import tpu as pltpu
from jax.sharding import PartitionSpec as P

masked_value = -1e30


def contract_last(left, right):
    return lax.dot_general(
        left, right, (((1,), (1,)), ((), ())), preferred_element_type=jnp.float32
    )


def contract_first(left, right):
    return lax.dot_general(
        left, right, (((0,), (0,)), ((), ())), preferred_element_type=jnp.float32
    )


def tile_scores(query_rows, query_gate, query_pos, key_rows, key_gate, key_pos, score_scale):
    scores = (
        contract_last(query_rows, key_rows) * score_scale + query_gate[:, None] - key_gate[None, :]
    )
    visible = key_pos[None, :] <= query_pos[:, None]
    return (scores, visible)


def tile_probs(scores, visible, row_total):
    return jnp.where(visible, jnp.exp(scores - row_total[:, None]), 0.0)


def local_general(queries, keys, values, log_gate, out_grad, segment_order):
    tokens_here, width = queries.shape
    devices = lax.axis_size("seq")
    segment_rows = tokens_here // 2
    total_len = tokens_here * devices
    score_scale = width ** (-0.5)
    offsets_in = lax.broadcasted_iota(jnp.int32, (1, segment_rows), 1)
    local_cum = jnp.cumsum(log_gate.reshape(2, segment_rows), axis=1)
    segment_total = local_cum[:, -1]
    segment_place = segment_order.astype(jnp.float32)
    own_pos = (segment_order[:, None] * segment_rows + offsets_in).reshape(-1)
    all_totals, all_place = (
        lax.all_gather(segment_total, "seq", axis=0, tiled=True),
        lax.all_gather(segment_place, "seq", axis=0, tiled=True),
    )
    earlier = (all_place[None, :] < segment_place[:, None]).astype(jnp.float32)
    own_offset = jnp.sum(earlier * all_totals[None, :], axis=1)
    own_gate = (local_cum + own_offset[:, None]).reshape(-1)
    all_gate = lax.all_gather(own_gate, "seq", axis=0, tiled=True)
    all_pos = (all_place.astype(jnp.int32)[:, None] * segment_rows + offsets_in).reshape(-1)
    key_all, value_all = (
        lax.all_gather(keys, "seq", axis=0, tiled=True),
        lax.all_gather(values, "seq", axis=0, tiled=True),
    )
    block = 2048
    count = total_len // block

    def key_tile(block_index):
        start = block_index * block
        return (
            lax.dynamic_slice_in_dim(key_all, start, block),
            lax.dynamic_slice_in_dim(value_all, start, block),
            lax.dynamic_slice_in_dim(all_gate, start, block),
            lax.dynamic_slice_in_dim(all_pos, start, block),
        )

    def stats_step(block_index, carry):
        run_max, run_sum = carry
        key_rows, value_rows, key_gate, key_pos = key_tile(block_index)
        scores, visible = tile_scores(
            queries, own_gate, own_pos, key_rows, key_gate, key_pos, score_scale
        )
        kept = jnp.where(visible, scores, masked_value)
        new_max = jnp.maximum(run_max, jnp.max(kept, axis=1))
        fresh = jnp.sum(jnp.where(visible, jnp.exp(kept - new_max[:, None]), 0.0), axis=1)
        return (new_max, run_sum * jnp.exp(run_max - new_max) + fresh)

    start_max = jnp.full((tokens_here,), masked_value, jnp.float32)
    run_max, run_sum = lax.fori_loop(
        0, count, stats_step, (start_max, jnp.zeros((tokens_here,), jnp.float32))
    )
    log_total = run_max + jnp.log(run_sum)

    def output_step(block_index, total):
        key_rows, value_rows, key_gate, key_pos = key_tile(block_index)
        scores, visible = tile_scores(
            queries, own_gate, own_pos, key_rows, key_gate, key_pos, score_scale
        )
        probs = tile_probs(scores, visible, log_total).astype(jnp.bfloat16)
        return total + jnp.dot(probs, value_rows, preferred_element_type=jnp.float32)

    out_full = lax.fori_loop(0, count, output_step, jnp.zeros((tokens_here, width), jnp.float32))
    attn_out = out_full.astype(jnp.bfloat16)
    row_delta = jnp.sum(out_grad.astype(jnp.float32) * out_full, axis=1)

    def row_terms(block_index):
        key_rows, value_rows, key_gate, key_pos = key_tile(block_index)
        scores, visible = tile_scores(
            queries, own_gate, own_pos, key_rows, key_gate, key_pos, score_scale
        )
        probs = tile_probs(scores, visible, log_total)
        dprob = contract_last(out_grad, value_rows)
        return (key_rows, probs, probs * (dprob - row_delta[:, None]))

    def query_step(block_index, total):
        key_rows, probs, dscore = row_terms(block_index)
        return total + jnp.dot(
            dscore.astype(jnp.bfloat16), key_rows, preferred_element_type=jnp.float32
        )

    query_acc = lax.fori_loop(0, count, query_step, jnp.zeros((tokens_here, width), jnp.float32))
    query_all, grad_all = (
        lax.all_gather(queries, "seq", axis=0, tiled=True),
        lax.all_gather(out_grad, "seq", axis=0, tiled=True),
    )
    total_all, delta_all = (
        lax.all_gather(log_total, "seq", axis=0, tiled=True),
        lax.all_gather(row_delta, "seq", axis=0, tiled=True),
    )

    def column_step(block_index, carry):
        key_acc, value_acc, column_acc = carry
        start = block_index * block
        query_rows = lax.dynamic_slice_in_dim(query_all, start, block)
        grad_rows = lax.dynamic_slice_in_dim(grad_all, start, block)
        scores, visible = tile_scores(
            query_rows,
            lax.dynamic_slice_in_dim(all_gate, start, block),
            lax.dynamic_slice_in_dim(all_pos, start, block),
            keys,
            own_gate,
            own_pos,
            score_scale,
        )
        probs = tile_probs(scores, visible, lax.dynamic_slice_in_dim(total_all, start, block))
        dprob = contract_last(grad_rows, values)
        dscore = probs * (dprob - lax.dynamic_slice_in_dim(delta_all, start, block)[:, None])
        dscore_low = dscore.astype(jnp.bfloat16)
        key_acc = key_acc + contract_first(dscore_low, query_rows) * score_scale
        value_acc = value_acc + contract_first(probs.astype(jnp.bfloat16), grad_rows)
        column_acc = column_acc - jnp.sum(dscore, axis=0)
        return (key_acc, value_acc, column_acc)

    zeros_own = jnp.zeros((tokens_here, width), jnp.float32)
    key_grad, value_grad, gate_point = lax.fori_loop(
        0, count, column_step, (zeros_own, zeros_own, jnp.zeros((tokens_here,), jnp.float32))
    )
    query_grad = query_acc * score_scale
    point_rows = gate_point.reshape(2, segment_rows)
    within = jnp.flip(jnp.cumsum(jnp.flip(point_rows, 1), axis=1), 1)
    all_point = lax.all_gather(within[:, 0], "seq", axis=0, tiled=True)
    later = (all_place[None, :] > segment_place[:, None]).astype(jnp.float32)
    gate_grad = (within + jnp.sum(later * all_point[None, :], axis=1)[:, None]).reshape(-1)
    return (attn_out, query_grad, key_grad, value_grad, gate_grad)


LOG2E = 1.4426950408889634
META = 16
ROWS = 256


def pack_kernel(q_ref, k_ref, v_ref, g_ref, gate_ref, order_ref, out_ref):
    tokens = q_ref.shape[0]
    out_ref[0:tokens] = q_ref[...]
    out_ref[tokens : 2 * tokens] = k_ref[...]
    out_ref[2 * tokens : 3 * tokens] = v_ref[...]
    out_ref[3 * tokens : 4 * tokens] = g_ref[...]
    gate = gate_ref[...]
    high = gate.astype(jnp.bfloat16).astype(jnp.float32)
    rest = gate - high
    mid = rest.astype(jnp.bfloat16).astype(jnp.float32)
    low = rest - mid
    lane = lax.broadcasted_iota(jnp.int32, (META, tokens), 1)
    row = lax.broadcasted_iota(jnp.int32, (META, tokens), 0)
    order = order_ref[...].astype(jnp.float32)
    place = jnp.where(lane < tokens // 2, order[:, 0:1], order[:, 1:2])
    meta = jnp.where(
        row == 0, high, jnp.where(row == 1, mid, jnp.where(row == 2, low, place))
    )
    out_ref[4 * tokens : 4 * tokens + META] = meta.astype(jnp.bfloat16)


def roll_sum_lanes(x, span, reverse):
    lanes = x.shape[1]
    lane = lax.broadcasted_iota(jnp.int32, x.shape, 1)
    step = 1
    while step < span:
        if reverse:
            x = x + jnp.where(lane < lanes - step, pltpu.roll(x, lanes - step, 1), 0.0)
        else:
            x = x + jnp.where(lane >= step, pltpu.roll(x, step, 1), 0.0)
        step *= 2
    return x


def roll_sum_rows(x, reverse):
    rows = x.shape[0]
    row = lax.broadcasted_iota(jnp.int32, x.shape, 0)
    step = 1
    while step < rows:
        if reverse:
            x = x + jnp.where(row < rows - step, pltpu.roll(x, rows - step, 0), 0.0)
        else:
            x = x + jnp.where(row >= step, pltpu.roll(x, step, 0), 0.0)
        step *= 2
    return x


def core_kernel(counts, tokens, width, *refs):
    blocks = refs[: len(counts)]
    out_ref, dq_ref, dk_ref, dv_ref, gate_ref = refs[len(counts) : len(counts) + 5]
    (qs, ks, vs, gs, cums, key_row, scores, top_col, inv_col, delta_col, outs, points,
     point_rows) = refs[len(counts) + 5 :]
    seg = tokens // 2
    total = qs.shape[0]
    segments = total // seg
    size = 4 * tokens + META
    scale = width ** (-0.5)
    lane1 = lax.broadcasted_iota(jnp.int32, (1, tokens), 1)
    left = lane1 < seg

    own_place = None
    for ref, count in zip(blocks, counts):
        for index in range(count):
            base = index * size
            meta = ref[base + 4 * tokens : base + size].astype(jnp.float32)
            gate = (meta[0:1] + meta[1:2]) + meta[2:3]
            place = meta[3:4].astype(jnp.int32)
            pair = (place[0, 0], place[0, seg])
            if own_place is None:
                own_place = pair
            for half in range(2):
                at = pl.multiple_of(pair[half] * seg, seg)
                for slot, dest in enumerate((qs, ks, vs, gs)):
                    first = base + slot * tokens + half * seg
                    dest[pl.ds(at, seg), :] = ref[first : first + seg, :]
                shifted = gate if half == 0 else pltpu.roll(gate, seg, 1)
                cums[pl.ds(pair[half], 1), :] = jnp.where(left, shifted, 0.0)

    inside = roll_sum_lanes(cums[...], seg, False)
    whole = jnp.broadcast_to(inside[:, seg - 1 : seg], inside.shape)
    before = roll_sum_rows(whole, False) - whole
    cums[...] = (inside + before) * LOG2E
    for tile in range(segments // 2):
        even = cums[2 * tile : 2 * tile + 1, :]
        odd = pltpu.roll(cums[2 * tile + 1 : 2 * tile + 2, :], seg, 1)
        key_row[:, tile * tokens : (tile + 1) * tokens] = jnp.where(left, even, odd)

    points[...] = jnp.zeros_like(points)
    block_rows = ROWS
    row_in = lax.broadcasted_iota(jnp.int32, (block_rows, block_rows), 0)
    col_in = lax.broadcasted_iota(jnp.int32, (block_rows, block_rows), 1)
    causal = col_in <= row_in
    for block in range(total // block_rows):
        r0 = block * block_rows
        q = qs[r0 : r0 + block_rows, :]
        g = gs[r0 : r0 + block_rows, :]
        best = None
        for tile in range(block + 1):
            c0 = tile * block_rows
            s = contract_last(q, ks[c0 : c0 + block_rows, :]) * (scale * LOG2E)
            s = s - key_row[:, c0 : c0 + block_rows]
            if tile == block:
                s = jnp.where(causal, s, masked_value)
            scores[:, c0 : c0 + block_rows] = s
            part = jnp.maximum(s[:, :128], s[:, 128:])
            best = part if best is None else jnp.maximum(best, part)
        top = jnp.max(best, axis=1, keepdims=True)
        mass = None
        for tile in range(block + 1):
            c0 = tile * block_rows
            e = jnp.exp2(scores[:, c0 : c0 + block_rows] - top)
            scores[:, c0 : c0 + block_rows] = e
            part = e[:, :128] + e[:, 128:]
            mass = part if mass is None else mass + part
        inv = 1.0 / jnp.sum(mass, axis=1, keepdims=True)
        acc = jnp.zeros((block_rows, width), jnp.float32)
        for tile in range(block + 1):
            c0 = tile * block_rows
            p = (scores[:, c0 : c0 + block_rows] * inv).astype(jnp.bfloat16)
            acc = acc + jnp.dot(p, vs[c0 : c0 + block_rows, :], preferred_element_type=jnp.float32)
        delta = jnp.sum(g.astype(jnp.float32) * acc, axis=1, keepdims=True)
        outs[r0 : r0 + block_rows, :] = acc
        top_col[r0 : r0 + block_rows, :] = top
        inv_col[r0 : r0 + block_rows, :] = inv
        delta_col[r0 : r0 + block_rows, :] = delta
        for tile in range(block + 1):
            c0 = tile * block_rows
            dp = contract_last(g, vs[c0 : c0 + block_rows, :])
            ds = (scores[:, c0 : c0 + block_rows] * inv) * (dp - delta)
            points[:, c0 : c0 + block_rows] += jnp.sum(
                ds.reshape(block_rows // 8, 8, block_rows), axis=0
            )

    for tile in range(segments // 2):
        c0 = tile * tokens
        point_rows[tile : tile + 1, :] = -jnp.sum(
            points[:, c0 : c0 + tokens], axis=0, keepdims=True
        )
    inside = roll_sum_lanes(point_rows[...], tokens, True)
    whole = jnp.broadcast_to(inside[:, 0:1], inside.shape)
    point_rows[...] = inside + (roll_sum_rows(whole, True) - whole)
    halves = []
    for half in range(2):
        line = point_rows[pl.ds(own_place[half] // 2, 1), :]
        turned = pltpu.roll(line, seg, 1)
        halves.append(jnp.where(own_place[half] % 2 == half, line, turned))
    gate_ref[...] = jnp.where(left, halves[0], halves[1])

    own = blocks[0]
    starts = [pl.multiple_of(p * seg, seg) for p in own_place]

    def pick(ref):
        return jnp.concatenate([ref[pl.ds(s, seg), :] for s in starts], axis=0)

    top, inv, delta = pick(top_col), pick(inv_col), pick(delta_col)
    out_ref[...] = pick(outs).astype(jnp.bfloat16)
    inner = lax.broadcasted_iota(jnp.int32, (tokens, 1), 0)
    row_pos = jnp.where(inner < seg, starts[0] + inner, starts[1] + inner - seg)
    chunk = 512
    q = own[0:tokens, :]
    k = own[tokens : 2 * tokens, :]
    v = own[2 * tokens : 3 * tokens, :]
    g = own[3 * tokens : 4 * tokens, :]
    acc = jnp.zeros((tokens, width), jnp.float32)
    for c0 in range(0, total, chunk):
        keys = ks[c0 : c0 + chunk, :]
        s = contract_last(q, keys) * (scale * LOG2E) - key_row[:, c0 : c0 + chunk]
        seen = lax.broadcasted_iota(jnp.int32, (tokens, chunk), 1) + c0 <= row_pos
        p = jnp.where(seen, jnp.exp2(s - top), 0.0) * inv
        ds = p * (contract_last(g, vs[c0 : c0 + chunk, :]) - delta)
        acc = acc + jnp.dot(ds.astype(jnp.bfloat16), keys, preferred_element_type=jnp.float32)
    dq_ref[...] = acc * scale

    rows = [cums[pl.ds(p, 1), :] for p in own_place]
    own_key = jnp.where(left, rows[0], pltpu.roll(rows[1], seg, 1))
    col_pos = jnp.where(left, starts[0] + lane1, starts[1] + lane1 - seg)
    acc_k = jnp.zeros((tokens, width), jnp.float32)
    acc_v = jnp.zeros((tokens, width), jnp.float32)
    for r0 in range(0, total, chunk):
        queries = qs[r0 : r0 + chunk, :]
        grads = gs[r0 : r0 + chunk, :]
        s = contract_last(queries, k) * (scale * LOG2E) - own_key
        seen = lax.broadcasted_iota(jnp.int32, (chunk, tokens), 0) + r0 >= col_pos
        p = jnp.where(seen, jnp.exp2(s - top_col[r0 : r0 + chunk, :]), 0.0)
        p = p * inv_col[r0 : r0 + chunk, :]
        ds = p * (contract_last(grads, v) - delta_col[r0 : r0 + chunk, :])
        acc_v = acc_v + contract_first(p.astype(jnp.bfloat16), grads)
        acc_k = acc_k + contract_first(ds.astype(jnp.bfloat16), queries)
    dk_ref[...] = acc_k * scale
    dv_ref[...] = acc_v


def core_call(blocks, tokens, width, devices):
    size = 4 * tokens + META
    counts = tuple(b.shape[0] // size for b in blocks)
    total = tokens * devices
    segments = 2 * devices
    vmem = pl.BlockSpec(memory_space=pltpu.VMEM)
    square = jax.ShapeDtypeStruct((tokens, width), jnp.float32)
    import functools

    return pl.pallas_call(
        functools.partial(core_kernel, counts, tokens, width),
        out_shape=(
            jax.ShapeDtypeStruct((tokens, width), jnp.bfloat16),
            square,
            square,
            square,
            jax.ShapeDtypeStruct((1, tokens), jnp.float32),
        ),
        in_specs=[vmem] * len(blocks),
        out_specs=[vmem] * 5,
        scratch_shapes=[pltpu.VMEM((total, width), jnp.bfloat16)] * 4
        + [
            pltpu.VMEM((segments, tokens), jnp.float32),
            pltpu.VMEM((1, total), jnp.float32),
            pltpu.VMEM((ROWS, total), jnp.float32),
            pltpu.VMEM((total, 1), jnp.float32),
            pltpu.VMEM((total, 1), jnp.float32),
            pltpu.VMEM((total, 1), jnp.float32),
            pltpu.VMEM((total, width), jnp.float32),
            pltpu.VMEM((8, total), jnp.float32),
            pltpu.VMEM((segments // 2, tokens), jnp.float32),
        ],
        name="core",
    )(*blocks)


def shift(x, devices, ring=0, flip=0):
    line = devices // 4
    pairs = []
    for i in range(devices):
        place, low = i // 4, i % 4
        pairs.append((i, ((place + ring) % line) * 4 + (low ^ flip)))
    return lax.ppermute(x, "seq", pairs)


def gather_blocks(x, devices):
    a = shift(x, devices, flip=2)
    b = shift(x, devices, ring=1)
    c = shift(x, devices, ring=-1)
    d = shift(c, devices, flip=2)
    e = shift(a, devices, ring=1)
    f = shift(c, devices, ring=-1)
    g = shift(f, devices, flip=2)
    near = [x, a, b, c, d, e, f, g]
    return near + [shift(t, devices, flip=1) for t in near]


def local_small(queries, keys, values, log_gate, out_grad, segment_order):
    tokens, width = queries.shape
    devices = lax.axis_size("seq")
    vmem = pl.BlockSpec(memory_space=pltpu.VMEM)
    packed = pl.pallas_call(
        pack_kernel,
        out_shape=jax.ShapeDtypeStruct((4 * tokens + META, width), jnp.bfloat16),
        in_specs=[vmem] * 6,
        out_specs=vmem,
        name="pack",
    )(queries, keys, values, out_grad, log_gate.reshape(1, tokens), segment_order.reshape(1, 2))
    blocks = gather_blocks(packed, devices)
    out, dq, dk, dv, gate = core_call(blocks, tokens, width, devices)
    return (out, dq, dk, dv, gate.reshape(tokens))


def local(queries, keys, values, log_gate, out_grad, segment_order):
    tokens, width = queries.shape
    small = tokens == 128 and width == 128 and lax.axis_size("seq") == 16
    path = local_small if small else local_general
    return path(queries, keys, values, log_gate, out_grad, segment_order)


def solution(mesh):
    placed = (
        P(("grp", "seq"), None),
        P(("grp", "seq"), None),
        P(("grp", "seq"), None),
        P(("grp", "seq")),
        P(("grp", "seq"), None),
        P(("grp", "seq")),
    )
    return jax.shard_map(
        local,
        mesh=mesh,
        in_specs=placed,
        out_specs=(
            P(("grp", "seq"), None),
            P(("grp", "seq"), None),
            P(("grp", "seq"), None),
            P(("grp", "seq"), None),
            P(("grp", "seq")),
        ),
        check_vma=False,
    )
```

```python
import jax
import jax.numpy as jnp
from jax import lax
from jax.experimental import pallas as pl
from jax.experimental.pallas import tpu as pltpu
from jax.sharding import PartitionSpec as P

masked_value = -1e30


def contract_last(left, right):
    return lax.dot_general(
        left, right, (((1,), (1,)), ((), ())), preferred_element_type=jnp.float32
    )


def contract_first(left, right):
    return lax.dot_general(
        left, right, (((0,), (0,)), ((), ())), preferred_element_type=jnp.float32
    )


def tile_scores(query_rows, query_gate, query_pos, key_rows, key_gate, key_pos, score_scale):
    scores = (
        contract_last(query_rows, key_rows) * score_scale + query_gate[:, None] - key_gate[None, :]
    )
    visible = key_pos[None, :] <= query_pos[:, None]
    return (scores, visible)


def tile_probs(scores, visible, row_total):
    return jnp.where(visible, jnp.exp(scores - row_total[:, None]), 0.0)


def local_general(queries, keys, values, log_gate, out_grad, segment_order):
    tokens_here, width = queries.shape
    devices = lax.axis_size("seq")
    segment_rows = tokens_here // 2
    total_len = tokens_here * devices
    score_scale = width ** (-0.5)
    offsets_in = lax.broadcasted_iota(jnp.int32, (1, segment_rows), 1)
    local_cum = jnp.cumsum(log_gate.reshape(2, segment_rows), axis=1)
    segment_total = local_cum[:, -1]
    segment_place = segment_order.astype(jnp.float32)
    own_pos = (segment_order[:, None] * segment_rows + offsets_in).reshape(-1)
    all_totals, all_place = (
        lax.all_gather(segment_total, "seq", axis=0, tiled=True),
        lax.all_gather(segment_place, "seq", axis=0, tiled=True),
    )
    earlier = (all_place[None, :] < segment_place[:, None]).astype(jnp.float32)
    own_offset = jnp.sum(earlier * all_totals[None, :], axis=1)
    own_gate = (local_cum + own_offset[:, None]).reshape(-1)
    all_gate = lax.all_gather(own_gate, "seq", axis=0, tiled=True)
    all_pos = (all_place.astype(jnp.int32)[:, None] * segment_rows + offsets_in).reshape(-1)
    key_all, value_all = (
        lax.all_gather(keys, "seq", axis=0, tiled=True),
        lax.all_gather(values, "seq", axis=0, tiled=True),
    )
    block = 2048
    count = total_len // block

    def key_tile(block_index):
        start = block_index * block
        return (
            lax.dynamic_slice_in_dim(key_all, start, block),
            lax.dynamic_slice_in_dim(value_all, start, block),
            lax.dynamic_slice_in_dim(all_gate, start, block),
            lax.dynamic_slice_in_dim(all_pos, start, block),
        )

    def stats_step(block_index, carry):
        run_max, run_sum = carry
        key_rows, value_rows, key_gate, key_pos = key_tile(block_index)
        scores, visible = tile_scores(
            queries, own_gate, own_pos, key_rows, key_gate, key_pos, score_scale
        )
        kept = jnp.where(visible, scores, masked_value)
        new_max = jnp.maximum(run_max, jnp.max(kept, axis=1))
        fresh = jnp.sum(jnp.where(visible, jnp.exp(kept - new_max[:, None]), 0.0), axis=1)
        return (new_max, run_sum * jnp.exp(run_max - new_max) + fresh)

    start_max = jnp.full((tokens_here,), masked_value, jnp.float32)
    run_max, run_sum = lax.fori_loop(
        0, count, stats_step, (start_max, jnp.zeros((tokens_here,), jnp.float32))
    )
    log_total = run_max + jnp.log(run_sum)

    def output_step(block_index, total):
        key_rows, value_rows, key_gate, key_pos = key_tile(block_index)
        scores, visible = tile_scores(
            queries, own_gate, own_pos, key_rows, key_gate, key_pos, score_scale
        )
        probs = tile_probs(scores, visible, log_total).astype(jnp.bfloat16)
        return total + jnp.dot(probs, value_rows, preferred_element_type=jnp.float32)

    out_full = lax.fori_loop(0, count, output_step, jnp.zeros((tokens_here, width), jnp.float32))
    attn_out = out_full.astype(jnp.bfloat16)
    row_delta = jnp.sum(out_grad.astype(jnp.float32) * out_full, axis=1)

    def row_terms(block_index):
        key_rows, value_rows, key_gate, key_pos = key_tile(block_index)
        scores, visible = tile_scores(
            queries, own_gate, own_pos, key_rows, key_gate, key_pos, score_scale
        )
        probs = tile_probs(scores, visible, log_total)
        dprob = contract_last(out_grad, value_rows)
        return (key_rows, probs, probs * (dprob - row_delta[:, None]))

    def query_step(block_index, total):
        key_rows, probs, dscore = row_terms(block_index)
        return total + jnp.dot(
            dscore.astype(jnp.bfloat16), key_rows, preferred_element_type=jnp.float32
        )

    query_acc = lax.fori_loop(0, count, query_step, jnp.zeros((tokens_here, width), jnp.float32))
    query_all, grad_all = (
        lax.all_gather(queries, "seq", axis=0, tiled=True),
        lax.all_gather(out_grad, "seq", axis=0, tiled=True),
    )
    total_all, delta_all = (
        lax.all_gather(log_total, "seq", axis=0, tiled=True),
        lax.all_gather(row_delta, "seq", axis=0, tiled=True),
    )

    def column_step(block_index, carry):
        key_acc, value_acc, column_acc = carry
        start = block_index * block
        query_rows = lax.dynamic_slice_in_dim(query_all, start, block)
        grad_rows = lax.dynamic_slice_in_dim(grad_all, start, block)
        scores, visible = tile_scores(
            query_rows,
            lax.dynamic_slice_in_dim(all_gate, start, block),
            lax.dynamic_slice_in_dim(all_pos, start, block),
            keys,
            own_gate,
            own_pos,
            score_scale,
        )
        probs = tile_probs(scores, visible, lax.dynamic_slice_in_dim(total_all, start, block))
        dprob = contract_last(grad_rows, values)
        dscore = probs * (dprob - lax.dynamic_slice_in_dim(delta_all, start, block)[:, None])
        dscore_low = dscore.astype(jnp.bfloat16)
        key_acc = key_acc + contract_first(dscore_low, query_rows) * score_scale
        value_acc = value_acc + contract_first(probs.astype(jnp.bfloat16), grad_rows)
        column_acc = column_acc - jnp.sum(dscore, axis=0)
        return (key_acc, value_acc, column_acc)

    zeros_own = jnp.zeros((tokens_here, width), jnp.float32)
    key_grad, value_grad, gate_point = lax.fori_loop(
        0, count, column_step, (zeros_own, zeros_own, jnp.zeros((tokens_here,), jnp.float32))
    )
    query_grad = query_acc * score_scale
    point_rows = gate_point.reshape(2, segment_rows)
    within = jnp.flip(jnp.cumsum(jnp.flip(point_rows, 1), axis=1), 1)
    all_point = lax.all_gather(within[:, 0], "seq", axis=0, tiled=True)
    later = (all_place[None, :] > segment_place[:, None]).astype(jnp.float32)
    gate_grad = (within + jnp.sum(later * all_point[None, :], axis=1)[:, None]).reshape(-1)
    return (attn_out, query_grad, key_grad, value_grad, gate_grad)


LOG2E = 1.4426950408889634
META = 16
ROWS = 256


def pack_kernel(q_ref, k_ref, v_ref, g_ref, gate_ref, order_ref, out_ref):
    tokens = q_ref.shape[0]
    out_ref[0:tokens] = q_ref[...]
    out_ref[tokens : 2 * tokens] = k_ref[...]
    out_ref[2 * tokens : 3 * tokens] = v_ref[...]
    out_ref[3 * tokens : 4 * tokens] = g_ref[...]
    gate = gate_ref[...]
    high = gate.astype(jnp.bfloat16).astype(jnp.float32)
    rest = gate - high
    mid = rest.astype(jnp.bfloat16).astype(jnp.float32)
    low = rest - mid
    lane = lax.broadcasted_iota(jnp.int32, (META, tokens), 1)
    row = lax.broadcasted_iota(jnp.int32, (META, tokens), 0)
    order = order_ref[...].astype(jnp.float32)
    place = jnp.where(lane < tokens // 2, order[:, 0:1], order[:, 1:2])
    meta = jnp.where(
        row == 0, high, jnp.where(row == 1, mid, jnp.where(row == 2, low, place))
    )
    out_ref[4 * tokens : 4 * tokens + META] = meta.astype(jnp.bfloat16)


def roll_sum_lanes(x, span, reverse):
    lanes = x.shape[1]
    lane = lax.broadcasted_iota(jnp.int32, x.shape, 1)
    step = 1
    while step < span:
        if reverse:
            x = x + jnp.where(lane < lanes - step, pltpu.roll(x, lanes - step, 1), 0.0)
        else:
            x = x + jnp.where(lane >= step, pltpu.roll(x, step, 1), 0.0)
        step *= 2
    return x


def roll_sum_rows(x, reverse):
    rows = x.shape[0]
    row = lax.broadcasted_iota(jnp.int32, x.shape, 0)
    step = 1
    while step < rows:
        if reverse:
            x = x + jnp.where(row < rows - step, pltpu.roll(x, rows - step, 0), 0.0)
        else:
            x = x + jnp.where(row >= step, pltpu.roll(x, step, 0), 0.0)
        step *= 2
    return x


def core_kernel(counts, tokens, width, *refs):
    blocks = refs[: len(counts)]
    out_ref, dq_ref, dk_ref, dv_ref, gate_ref = refs[len(counts) : len(counts) + 5]
    (qs, ks, vs, gs, cums, key_row, scores, dprobs, probs, own_scores, own_dprobs, top_col, inv_col,
     delta_col, outs, points, point_rows) = refs[len(counts) + 5 :]
    seg = tokens // 2
    total = qs.shape[0]
    segments = total // seg
    size = 4 * tokens + META
    scale = width ** (-0.5)
    lane1 = lax.broadcasted_iota(jnp.int32, (1, tokens), 1)
    left = lane1 < seg

    own_place = None
    for ref, count in zip(blocks, counts):
        for index in range(count):
            base = index * size
            meta = ref[base + 4 * tokens : base + size].astype(jnp.float32)
            gate = (meta[0:1] + meta[1:2]) + meta[2:3]
            place = meta[3:4].astype(jnp.int32)
            pair = (place[0, 0], place[0, seg])
            if own_place is None:
                own_place = pair
            for half in range(2):
                at = pl.multiple_of(pair[half] * seg, seg)
                for slot, dest in enumerate((qs, ks, vs, gs)):
                    first = base + slot * tokens + half * seg
                    dest[pl.ds(at, seg), :] = ref[first : first + seg, :]
                shifted = gate if half == 0 else pltpu.roll(gate, seg, 1)
                cums[pl.ds(pair[half], 1), :] = jnp.where(left, shifted, 0.0)

    inside = roll_sum_lanes(cums[...], seg, False)
    whole = jnp.broadcast_to(inside[:, seg - 1 : seg], inside.shape)
    before = roll_sum_rows(whole, False) - whole
    cums[...] = (inside + before) * LOG2E
    for tile in range(segments // 2):
        even = cums[2 * tile : 2 * tile + 1, :]
        odd = pltpu.roll(cums[2 * tile + 1 : 2 * tile + 2, :], seg, 1)
        key_row[:, tile * tokens : (tile + 1) * tokens] = jnp.where(left, even, odd)

    points[...] = jnp.zeros_like(points)
    own = blocks[0]
    starts = [pl.multiple_of(p * seg, seg) for p in own_place]
    own_q = own[0:tokens, :]
    own_k = own[tokens : 2 * tokens, :]
    own_v = own[2 * tokens : 3 * tokens, :]
    own_g = own[3 * tokens : 4 * tokens, :]
    key_lines = [cums[pl.ds(p, 1), :] for p in own_place]
    own_key = jnp.where(left, key_lines[0], pltpu.roll(key_lines[1], seg, 1))
    col_pos = jnp.where(left, starts[0] + lane1, starts[1] + lane1 - seg)
    inner = lax.broadcasted_iota(jnp.int32, (tokens, 1), 0)
    row_pos = jnp.where(inner < seg, starts[0] + inner, starts[1] + inner - seg)
    dk_ref[...] = jnp.zeros_like(dk_ref)
    dv_ref[...] = jnp.zeros_like(dv_ref)

    size_r = ROWS
    blocks_r = total // size_r
    row_in = lax.broadcasted_iota(jnp.int32, (size_r, size_r), 0)
    col_in = lax.broadcasted_iota(jnp.int32, (size_r, size_r), 1)
    causal = col_in <= row_in
    factor = scale * LOG2E
    best = {}

    def rows_of(ref, block):
        return ref[block * size_r : (block + 1) * size_r, :]

    def score_tile(block, tile):
        c0 = tile * size_r
        s = contract_last(rows_of(qs, block), ks[c0 : c0 + size_r, :]) * factor
        s = s - key_row[:, c0 : c0 + size_r]
        if tile == block:
            s = jnp.where(causal, s, masked_value)
        scores[block % 2, :, c0 : c0 + size_r] = s
        part = s[:, :width]
        for at in range(width, size_r, width):
            part = jnp.maximum(part, s[:, at : at + width])
        best[block] = jnp.maximum(best[block], part) if block in best else part

    def own_row_tile(tile):
        c0 = tile * size_r
        s = contract_last(own_q, ks[c0 : c0 + size_r, :]) * factor - key_row[:, c0 : c0 + size_r]
        seen = lax.broadcasted_iota(jnp.int32, (tokens, size_r), 1) + c0 <= row_pos
        own_scores[:, c0 : c0 + size_r] = jnp.where(seen, s, masked_value)
        own_dprobs[:, c0 : c0 + size_r] = contract_last(own_g, vs[c0 : c0 + size_r, :])

    def exp_block(block):
        top = jnp.broadcast_to(jnp.max(best[block], axis=1, keepdims=True), (size_r, width))
        rows_of_top = top
        top_col[block * size_r : (block + 1) * size_r, :] = rows_of_top
        mass = None
        for tile in range(block + 1):
            c0 = tile * size_r
            dprobs[block % 2, :, c0 : c0 + size_r] = contract_last(
                rows_of(gs, block), vs[c0 : c0 + size_r, :]
            )
            for at in range(c0, c0 + size_r, width):
                e = jnp.exp2(scores[block % 2, :, at : at + width] - top)
                scores[block % 2, :, at : at + width] = e
                mass = e if mass is None else mass + e
        inv = jnp.broadcast_to(1.0 / jnp.sum(mass, axis=1, keepdims=True), (size_r, width))
        inv_col[block * size_r : (block + 1) * size_r, :] = inv

    for tile in range(1):
        score_tile(0, tile)
    exp_block(0)
    for block in range(blocks_r):
        r0 = block * size_r
        wide = r0 + size_r
        inv = rows_of(inv_col, block)
        for tile in range(block + 1):
            c0 = tile * size_r
            for at in range(c0, c0 + size_r, width):
                p = scores[block % 2, :, at : at + width] * inv
                scores[block % 2, :, at : at + width] = p
                probs[:, at : at + width] = p.astype(jnp.bfloat16)
            if block + 1 < blocks_r:
                score_tile(block + 1, tile)
        if block + 1 < blocks_r:
            score_tile(block + 1, block + 1)
        acc = jnp.dot(probs[:, :wide], vs[:wide, :], preferred_element_type=jnp.float32)
        outs[r0:wide, :] = acc
        own_row_tile(block)
        if block + 1 < blocks_r:
            exp_block(block + 1)
        g = rows_of(gs, block)
        delta = jnp.broadcast_to(
            jnp.sum(g.astype(jnp.float32) * acc, axis=1, keepdims=True), (size_r, width)
        )
        delta_col[r0:wide, :] = delta

        s = contract_last(rows_of(qs, block), own_k) * factor - own_key
        seen = lax.broadcasted_iota(jnp.int32, (size_r, tokens), 0) + r0 >= col_pos
        p = jnp.where(seen, jnp.exp2(s - rows_of(top_col, block)), 0.0) * inv
        ds = p * (contract_last(g, own_v) - delta)
        dv_ref[...] += contract_first(p.astype(jnp.bfloat16), g)
        dk_ref[...] += contract_first(ds.astype(jnp.bfloat16), rows_of(qs, block))

        for tile in range(block + 1):
            c0 = tile * size_r
            for at in range(c0, c0 + size_r, width):
                ds = scores[block % 2, :, at : at + width] * (
                    dprobs[block % 2, :, at : at + width] - delta
                )
                points[:, at : at + width] += jnp.sum(ds.reshape(size_r // 8, 8, width), axis=0)
    dk_ref[...] = dk_ref[...] * scale

    for tile in range(segments // 2):
        c0 = tile * tokens
        point_rows[tile : tile + 1, :] = -jnp.sum(
            points[:, c0 : c0 + tokens], axis=0, keepdims=True
        )
    inside = roll_sum_lanes(point_rows[...], tokens, True)
    whole = jnp.broadcast_to(inside[:, 0:1], inside.shape)
    point_rows[...] = inside + (roll_sum_rows(whole, True) - whole)
    halves = []
    for half in range(2):
        line = point_rows[pl.ds(own_place[half] // 2, 1), :]
        turned = pltpu.roll(line, seg, 1)
        halves.append(jnp.where(own_place[half] % 2 == half, line, turned))
    gate_ref[...] = jnp.where(left, halves[0], halves[1])

    def pick(ref):
        return jnp.concatenate([ref[pl.ds(s, seg), :] for s in starts], axis=0)

    top, inv, delta = pick(top_col), pick(inv_col), pick(delta_col)
    out_ref[...] = pick(outs).astype(jnp.bfloat16)
    for at in range(0, total, width):
        p = jnp.exp2(own_scores[:, at : at + width] - top) * inv
        ds = p * (own_dprobs[:, at : at + width] - delta)
        probs[0:tokens, at : at + width] = ds.astype(jnp.bfloat16)
    dq_ref[...] = jnp.dot(probs[0:tokens, :], ks[...], preferred_element_type=jnp.float32) * scale


def core_call(blocks, tokens, width, devices):
    size = 4 * tokens + META
    counts = tuple(b.shape[0] // size for b in blocks)
    total = tokens * devices
    segments = 2 * devices
    vmem = pl.BlockSpec(memory_space=pltpu.VMEM)
    square = jax.ShapeDtypeStruct((tokens, width), jnp.float32)
    import functools

    return pl.pallas_call(
        functools.partial(core_kernel, counts, tokens, width),
        out_shape=(
            jax.ShapeDtypeStruct((tokens, width), jnp.bfloat16),
            square,
            square,
            square,
            jax.ShapeDtypeStruct((1, tokens), jnp.float32),
        ),
        in_specs=[vmem] * len(blocks),
        out_specs=[vmem] * 5,
        scratch_shapes=[pltpu.VMEM((total, width), jnp.bfloat16)] * 4
        + [
            pltpu.VMEM((segments, tokens), jnp.float32),
            pltpu.VMEM((1, total), jnp.float32),
            pltpu.VMEM((2, ROWS, total), jnp.float32),
            pltpu.VMEM((2, ROWS, total), jnp.float32),
            pltpu.VMEM((ROWS, total), jnp.bfloat16),
            pltpu.VMEM((tokens, total), jnp.float32),
            pltpu.VMEM((tokens, total), jnp.float32),
            pltpu.VMEM((total, width), jnp.float32),
            pltpu.VMEM((total, width), jnp.float32),
            pltpu.VMEM((total, width), jnp.float32),
            pltpu.VMEM((total, width), jnp.float32),
            pltpu.VMEM((8, total), jnp.float32),
            pltpu.VMEM((segments // 2, tokens), jnp.float32),
        ],
        compiler_params=pltpu.CompilerParams(vmem_limit_bytes=32 * 2**20),
        name="core",
    )(*blocks)


def shift(x, devices, ring=0, flip=0):
    line = devices // 4
    pairs = []
    for i in range(devices):
        place, low = i // 4, i % 4
        pairs.append((i, ((place + ring) % line) * 4 + (low ^ flip)))
    return lax.ppermute(x, "seq", pairs)


def gather_blocks(x, devices):
    a = shift(x, devices, flip=2)
    b = shift(x, devices, ring=1)
    c = shift(x, devices, ring=-1)
    d = shift(c, devices, flip=2)
    e = shift(a, devices, ring=1)
    f = shift(c, devices, ring=-1)
    g = shift(f, devices, flip=2)
    near = [x, a, b, c, d, e, f, g]
    return near + [shift(t, devices, flip=1) for t in near]


def local_small(queries, keys, values, log_gate, out_grad, segment_order):
    tokens, width = queries.shape
    devices = lax.axis_size("seq")
    vmem = pl.BlockSpec(memory_space=pltpu.VMEM)
    packed = pl.pallas_call(
        pack_kernel,
        out_shape=jax.ShapeDtypeStruct((4 * tokens + META, width), jnp.bfloat16),
        in_specs=[vmem] * 6,
        out_specs=vmem,
        name="pack",
    )(queries, keys, values, out_grad, log_gate.reshape(1, tokens), segment_order.reshape(1, 2))
    blocks = gather_blocks(packed, devices)
    out, dq, dk, dv, gate = core_call(blocks, tokens, width, devices)
    return (out, dq, dk, dv, gate.reshape(tokens))


def local(queries, keys, values, log_gate, out_grad, segment_order):
    tokens, width = queries.shape
    small = tokens == 128 and width == 128 and lax.axis_size("seq") == 16
    path = local_small if small else local_general
    return path(queries, keys, values, log_gate, out_grad, segment_order)


def solution(mesh):
    placed = (
        P(("grp", "seq"), None),
        P(("grp", "seq"), None),
        P(("grp", "seq"), None),
        P(("grp", "seq")),
        P(("grp", "seq"), None),
        P(("grp", "seq")),
    )
    return jax.shard_map(
        local,
        mesh=mesh,
        in_specs=placed,
        out_specs=(
            P(("grp", "seq"), None),
            P(("grp", "seq"), None),
            P(("grp", "seq"), None),
            P(("grp", "seq"), None),
            P(("grp", "seq")),
        ),
        check_vma=False,
    )
```

```python
import jax
import jax.numpy as jnp
from jax import lax
from jax.experimental import pallas as pl
from jax.experimental.pallas import tpu as pltpu
from jax.sharding import PartitionSpec as P

masked_value = -1e30


def contract_last(left, right):
    return lax.dot_general(
        left, right, (((1,), (1,)), ((), ())), preferred_element_type=jnp.float32
    )


def contract_first(left, right):
    return lax.dot_general(
        left, right, (((0,), (0,)), ((), ())), preferred_element_type=jnp.float32
    )


def tile_scores(query_rows, query_gate, query_pos, key_rows, key_gate, key_pos, score_scale):
    scores = (
        contract_last(query_rows, key_rows) * score_scale + query_gate[:, None] - key_gate[None, :]
    )
    visible = key_pos[None, :] <= query_pos[:, None]
    return (scores, visible)


def tile_probs(scores, visible, row_total):
    return jnp.where(visible, jnp.exp(scores - row_total[:, None]), 0.0)


def local_general(queries, keys, values, log_gate, out_grad, segment_order):
    tokens_here, width = queries.shape
    devices = lax.axis_size("seq")
    segment_rows = tokens_here // 2
    total_len = tokens_here * devices
    score_scale = width ** (-0.5)
    offsets_in = lax.broadcasted_iota(jnp.int32, (1, segment_rows), 1)
    local_cum = jnp.cumsum(log_gate.reshape(2, segment_rows), axis=1)
    segment_total = local_cum[:, -1]
    segment_place = segment_order.astype(jnp.float32)
    own_pos = (segment_order[:, None] * segment_rows + offsets_in).reshape(-1)
    all_totals, all_place = (
        lax.all_gather(segment_total, "seq", axis=0, tiled=True),
        lax.all_gather(segment_place, "seq", axis=0, tiled=True),
    )
    earlier = (all_place[None, :] < segment_place[:, None]).astype(jnp.float32)
    own_offset = jnp.sum(earlier * all_totals[None, :], axis=1)
    own_gate = (local_cum + own_offset[:, None]).reshape(-1)
    all_gate = lax.all_gather(own_gate, "seq", axis=0, tiled=True)
    all_pos = (all_place.astype(jnp.int32)[:, None] * segment_rows + offsets_in).reshape(-1)
    key_all, value_all = (
        lax.all_gather(keys, "seq", axis=0, tiled=True),
        lax.all_gather(values, "seq", axis=0, tiled=True),
    )
    block = 2048
    count = total_len // block

    def key_tile(block_index):
        start = block_index * block
        return (
            lax.dynamic_slice_in_dim(key_all, start, block),
            lax.dynamic_slice_in_dim(value_all, start, block),
            lax.dynamic_slice_in_dim(all_gate, start, block),
            lax.dynamic_slice_in_dim(all_pos, start, block),
        )

    def stats_step(block_index, carry):
        run_max, run_sum = carry
        key_rows, value_rows, key_gate, key_pos = key_tile(block_index)
        scores, visible = tile_scores(
            queries, own_gate, own_pos, key_rows, key_gate, key_pos, score_scale
        )
        kept = jnp.where(visible, scores, masked_value)
        new_max = jnp.maximum(run_max, jnp.max(kept, axis=1))
        fresh = jnp.sum(jnp.where(visible, jnp.exp(kept - new_max[:, None]), 0.0), axis=1)
        return (new_max, run_sum * jnp.exp(run_max - new_max) + fresh)

    start_max = jnp.full((tokens_here,), masked_value, jnp.float32)
    run_max, run_sum = lax.fori_loop(
        0, count, stats_step, (start_max, jnp.zeros((tokens_here,), jnp.float32))
    )
    log_total = run_max + jnp.log(run_sum)

    def output_step(block_index, total):
        key_rows, value_rows, key_gate, key_pos = key_tile(block_index)
        scores, visible = tile_scores(
            queries, own_gate, own_pos, key_rows, key_gate, key_pos, score_scale
        )
        probs = tile_probs(scores, visible, log_total).astype(jnp.bfloat16)
        return total + jnp.dot(probs, value_rows, preferred_element_type=jnp.float32)

    out_full = lax.fori_loop(0, count, output_step, jnp.zeros((tokens_here, width), jnp.float32))
    attn_out = out_full.astype(jnp.bfloat16)
    row_delta = jnp.sum(out_grad.astype(jnp.float32) * out_full, axis=1)

    def row_terms(block_index):
        key_rows, value_rows, key_gate, key_pos = key_tile(block_index)
        scores, visible = tile_scores(
            queries, own_gate, own_pos, key_rows, key_gate, key_pos, score_scale
        )
        probs = tile_probs(scores, visible, log_total)
        dprob = contract_last(out_grad, value_rows)
        return (key_rows, probs, probs * (dprob - row_delta[:, None]))

    def query_step(block_index, total):
        key_rows, probs, dscore = row_terms(block_index)
        return total + jnp.dot(
            dscore.astype(jnp.bfloat16), key_rows, preferred_element_type=jnp.float32
        )

    query_acc = lax.fori_loop(0, count, query_step, jnp.zeros((tokens_here, width), jnp.float32))
    query_all, grad_all = (
        lax.all_gather(queries, "seq", axis=0, tiled=True),
        lax.all_gather(out_grad, "seq", axis=0, tiled=True),
    )
    total_all, delta_all = (
        lax.all_gather(log_total, "seq", axis=0, tiled=True),
        lax.all_gather(row_delta, "seq", axis=0, tiled=True),
    )

    def column_step(block_index, carry):
        key_acc, value_acc, column_acc = carry
        start = block_index * block
        query_rows = lax.dynamic_slice_in_dim(query_all, start, block)
        grad_rows = lax.dynamic_slice_in_dim(grad_all, start, block)
        scores, visible = tile_scores(
            query_rows,
            lax.dynamic_slice_in_dim(all_gate, start, block),
            lax.dynamic_slice_in_dim(all_pos, start, block),
            keys,
            own_gate,
            own_pos,
            score_scale,
        )
        probs = tile_probs(scores, visible, lax.dynamic_slice_in_dim(total_all, start, block))
        dprob = contract_last(grad_rows, values)
        dscore = probs * (dprob - lax.dynamic_slice_in_dim(delta_all, start, block)[:, None])
        dscore_low = dscore.astype(jnp.bfloat16)
        key_acc = key_acc + contract_first(dscore_low, query_rows) * score_scale
        value_acc = value_acc + contract_first(probs.astype(jnp.bfloat16), grad_rows)
        column_acc = column_acc - jnp.sum(dscore, axis=0)
        return (key_acc, value_acc, column_acc)

    zeros_own = jnp.zeros((tokens_here, width), jnp.float32)
    key_grad, value_grad, gate_point = lax.fori_loop(
        0, count, column_step, (zeros_own, zeros_own, jnp.zeros((tokens_here,), jnp.float32))
    )
    query_grad = query_acc * score_scale
    point_rows = gate_point.reshape(2, segment_rows)
    within = jnp.flip(jnp.cumsum(jnp.flip(point_rows, 1), axis=1), 1)
    all_point = lax.all_gather(within[:, 0], "seq", axis=0, tiled=True)
    later = (all_place[None, :] > segment_place[:, None]).astype(jnp.float32)
    gate_grad = (within + jnp.sum(later * all_point[None, :], axis=1)[:, None]).reshape(-1)
    return (attn_out, query_grad, key_grad, value_grad, gate_grad)


LOG2E = 1.4426950408889634
META = 16
ROWS = 256
COLS = 256


def pack_kernel(q_ref, k_ref, v_ref, g_ref, gate_hbm, order_hbm, out_ref, gate_ref, order_ref, sems):
    tokens = q_ref.shape[0]
    copies = [
        pltpu.make_async_copy(gate_hbm, gate_ref, sems.at[0]),
        pltpu.make_async_copy(order_hbm, order_ref, sems.at[1]),
    ]
    for index, ref in enumerate((q_ref, k_ref, v_ref, g_ref)):
        copies.append(
            pltpu.make_async_copy(
                ref, out_ref.at[pl.ds(index * tokens, tokens), :], sems.at[index + 2]
            )
        )
    for copy in copies:
        copy.start()
    copies[0].wait()
    copies[1].wait()
    gate = gate_ref[...]
    high = gate.astype(jnp.bfloat16).astype(jnp.float32)
    rest = gate - high
    mid = rest.astype(jnp.bfloat16).astype(jnp.float32)
    low = rest - mid
    lane = lax.broadcasted_iota(jnp.int32, (META, tokens), 1)
    row = lax.broadcasted_iota(jnp.int32, (META, tokens), 0)
    order = order_ref[...].astype(jnp.float32)
    place = jnp.where(lane < tokens // 2, order[:, 0:1], order[:, 1:2])
    meta = jnp.where(
        row == 0, high, jnp.where(row == 1, mid, jnp.where(row == 2, low, place))
    )
    out_ref[4 * tokens : 4 * tokens + META] = meta.astype(jnp.bfloat16)
    for copy in copies[2:]:
        copy.wait()


def split(items, turn, turns):
    return items[len(items) * turn // turns : len(items) * (turn + 1) // turns]


def roll_sum_lanes(x, span, reverse):
    lanes = x.shape[1]
    lane = lax.broadcasted_iota(jnp.int32, x.shape, 1)
    step = 1
    while step < span:
        if reverse:
            x = x + jnp.where(lane < lanes - step, pltpu.roll(x, lanes - step, 1), 0.0)
        else:
            x = x + jnp.where(lane >= step, pltpu.roll(x, step, 1), 0.0)
        step *= 2
    return x


def roll_sum_rows(x, reverse):
    rows = x.shape[0]
    row = lax.broadcasted_iota(jnp.int32, x.shape, 0)
    step = 1
    while step < rows:
        if reverse:
            x = x + jnp.where(row < rows - step, pltpu.roll(x, rows - step, 0), 0.0)
        else:
            x = x + jnp.where(row >= step, pltpu.roll(x, step, 0), 0.0)
        step *= 2
    return x


def core_kernel(counts, tokens, width, *refs):
    blocks = refs[: len(counts)]
    out_ref, dq_ref, dk_ref, dv_ref, gate_ref = refs[len(counts) : len(counts) + 5]
    (qs, ks, vs, gs, cums, key_row, scores, probs, own_scores, own_dprobs, total_col, delta_col,
     outs, points, point_rows) = refs[len(counts) + 5 :]
    seg = tokens // 2
    total = qs.shape[0]
    segments = total // seg
    size = 4 * tokens + META
    scale = width ** (-0.5)
    lane1 = lax.broadcasted_iota(jnp.int32, (1, tokens), 1)
    left = lane1 < seg

    own_place = None
    for ref, count in zip(blocks, counts):
        for index in range(count):
            base = index * size
            meta = ref[base + 4 * tokens : base + size].astype(jnp.float32)
            gate = (meta[0:1] + meta[1:2]) + meta[2:3]
            place = meta[3:4].astype(jnp.int32)
            pair = (place[0, 0], place[0, seg])
            if own_place is None:
                own_place = pair
            for half in range(2):
                at = pl.multiple_of(pair[half] * seg, seg)
                for slot, dest in enumerate((qs, ks, vs, gs)):
                    first = base + slot * tokens + half * seg
                    dest[pl.ds(at, seg), :] = ref[first : first + seg, :]
                shifted = gate if half == 0 else pltpu.roll(gate, seg, 1)
                cums[pl.ds(pair[half], 1), :] = jnp.where(left, shifted, 0.0)

    inside = roll_sum_lanes(cums[...], seg, False)
    whole = jnp.broadcast_to(inside[:, seg - 1 : seg], inside.shape)
    before = roll_sum_rows(whole, False) - whole
    cums[...] = (inside + before) * LOG2E
    for tile in range(segments // 2):
        even = cums[2 * tile : 2 * tile + 1, :]
        odd = pltpu.roll(cums[2 * tile + 1 : 2 * tile + 2, :], seg, 1)
        key_row[:, tile * tokens : (tile + 1) * tokens] = jnp.where(left, even, odd)

    points[...] = jnp.zeros_like(points)
    own = blocks[0]
    starts = [pl.multiple_of(p * seg, seg) for p in own_place]
    own_q = own[0:tokens, :]
    own_k = own[tokens : 2 * tokens, :]
    own_v = own[2 * tokens : 3 * tokens, :]
    own_g = own[3 * tokens : 4 * tokens, :]
    key_lines = [cums[pl.ds(p, 1), :] for p in own_place]
    own_key = jnp.where(left, key_lines[0], pltpu.roll(key_lines[1], seg, 1))
    col_pos = jnp.where(left, starts[0] + lane1, starts[1] + lane1 - seg)
    inner = lax.broadcasted_iota(jnp.int32, (tokens, 1), 0)
    row_pos = jnp.where(inner < seg, starts[0] + inner, starts[1] + inner - seg)
    dk_ref[...] = jnp.zeros_like(dk_ref)
    dv_ref[...] = jnp.zeros_like(dv_ref)

    size_r, size_c = ROWS, COLS
    blocks_r = total // size_r
    row_in = lax.broadcasted_iota(jnp.int32, (size_r, size_c), 0)
    col_in = lax.broadcasted_iota(jnp.int32, (size_r, size_c), 1)
    causal = [col_in <= row_in + at for at in range(0, max(size_c, size_r), size_r)]
    factor = scale * LOG2E
    best = {}
    slots = {}

    def rows_of(ref, block):
        return ref[block * size_r : (block + 1) * size_r, :]

    def spread(column):
        return jnp.broadcast_to(column, (column.shape[0], width))

    def tiles_of(block):
        return range(((block + 1) * size_r + size_c - 1) // size_c)

    def score_tile(block, tile):
        c0 = tile * size_c
        s = contract_last(rows_of(qs, block), ks[c0 : c0 + size_c, :]) * factor
        s = s - key_row[:, c0 : c0 + size_c]
        if c0 + size_c > block * size_r:
            s = jnp.where(causal[block % len(causal)], s, masked_value)
        scores[slots[block], :, c0 : c0 + size_c] = s
        part = s[:, :width]
        for at in range(width, size_c, width):
            part = jnp.maximum(part, s[:, at : at + width])
        best[block] = jnp.maximum(best[block], part) if block in best else part

    def own_row_tile(tile):
        c0 = tile * size_c
        s = contract_last(own_q, ks[c0 : c0 + size_c, :]) * factor - key_row[:, c0 : c0 + size_c]
        seen = lax.broadcasted_iota(jnp.int32, (tokens, size_c), 1) + c0 <= row_pos
        own_scores[:, c0 : c0 + size_c] = jnp.where(seen, s, masked_value)
        own_dprobs[:, c0 : c0 + size_c] = contract_last(own_g, vs[c0 : c0 + size_c, :])

    def totals(block):
        top = spread(jnp.max(best[block], axis=1, keepdims=True))
        mass = None
        for at in range(0, len(tiles_of(block)) * size_c, width):
            e = jnp.exp2(scores[slots[block], :, at : at + width] - top)
            mass = e if mass is None else mass + e
        total_col[block * size_r : (block + 1) * size_r, :] = top + spread(
            jnp.log2(jnp.sum(mass, axis=1, keepdims=True))
        )

    def prob_tile(block, tile, low):
        log_total = rows_of(total_col, block)
        for at in range(tile * size_c, (tile + 1) * size_c, width):
            p = jnp.exp2(scores[slots[block], :, at : at + width] - log_total)
            probs[slots[block], :, at : at + width] = p
            low.append(p.astype(jnp.bfloat16))

    def outputs(block, low):
        wide = len(tiles_of(block)) * size_c
        acc = jnp.dot(
            jnp.concatenate(low, axis=1), vs[:wide, :], preferred_element_type=jnp.float32
        )
        outs[block * size_r : (block + 1) * size_r, :] = acc
        g = rows_of(gs, block).astype(jnp.float32)
        delta_col[block * size_r : (block + 1) * size_r, :] = spread(
            jnp.sum(g * acc, axis=1, keepdims=True)
        )

    def own_cols(block):
        r0 = block * size_r
        g = rows_of(gs, block)
        s = contract_last(rows_of(qs, block), own_k) * factor - own_key
        seen = lax.broadcasted_iota(jnp.int32, (size_r, tokens), 0) + r0 >= col_pos
        p = jnp.where(seen, jnp.exp2(s - rows_of(total_col, block)), 0.0)
        ds = p * (contract_last(g, own_v) - rows_of(delta_col, block))
        dv_ref[...] += contract_first(p.astype(jnp.bfloat16), g)
        dk_ref[...] += contract_first(ds.astype(jnp.bfloat16), rows_of(qs, block))

    def point_tile(block, tile):
        c0 = tile * size_c
        delta = rows_of(delta_col, block)
        dp = contract_last(rows_of(gs, block), vs[c0 : c0 + size_c, :])
        for at in range(0, size_c, width):
            ds = probs[slots[block], :, c0 + at : c0 + at + width] * (dp[:, at : at + width] - delta)
            points[:, c0 + at : c0 + at + width] += jnp.sum(
                ds.reshape(size_r // 8, 8, width), axis=0
            )

    rest = list(range(1, blocks_r))
    sequence = []
    while rest:
        sequence.append(rest.pop(0))
        if rest:
            sequence.append(rest.pop())
    sequence.append(0)
    slots.update({block: step % 2 for step, block in enumerate(sequence)})
    first = sequence[0]
    for tile in tiles_of(first):
        score_tile(first, tile)
    totals(first)
    row_tiles = list(range(total // size_c))
    for step, block in enumerate(sequence):
        after = sequence[step + 1] if step + 1 < blocks_r else None
        ahead = list(tiles_of(after)) if after is not None else []
        here = list(tiles_of(block))
        low = []
        for turn in range(max(len(here), len(ahead))):
            for tile in split(ahead, turn, max(len(here), len(ahead))):
                score_tile(after, tile)
            for tile in split(here, turn, max(len(here), len(ahead))):
                prob_tile(block, tile, low)
        outputs(block, low)
        if after is not None:
            totals(after)
        if row_tiles and step % max(1, blocks_r // (total // size_c)) == 0:
            own_row_tile(row_tiles.pop(0))
        own_cols(block)
        for tile in here:
            point_tile(block, tile)
    dk_ref[...] = dk_ref[...] * scale

    for tile in range(segments // 2):
        c0 = tile * tokens
        point_rows[tile : tile + 1, :] = -jnp.sum(
            points[:, c0 : c0 + tokens], axis=0, keepdims=True
        )
    inside = roll_sum_lanes(point_rows[...], tokens, True)
    whole = jnp.broadcast_to(inside[:, 0:1], inside.shape)
    point_rows[...] = inside + (roll_sum_rows(whole, True) - whole)
    halves = []
    for half in range(2):
        line = point_rows[pl.ds(own_place[half] // 2, 1), :]
        turned = pltpu.roll(line, seg, 1)
        halves.append(jnp.where(own_place[half] % 2 == half, line, turned))
    gate_ref[...] = jnp.where(left, halves[0], halves[1])

    def pick(ref):
        return jnp.concatenate([ref[pl.ds(s, seg), :] for s in starts], axis=0)

    log_total, delta = pick(total_col), pick(delta_col)
    out_ref[...] = pick(outs).astype(jnp.bfloat16)
    low = []
    for at in range(0, total, width):
        p = jnp.exp2(own_scores[:, at : at + width] - log_total)
        ds = p * (own_dprobs[:, at : at + width] - delta)
        low.append(ds.astype(jnp.bfloat16))
    dq_ref[...] = scale * jnp.dot(
        jnp.concatenate(low, axis=1), ks[...], preferred_element_type=jnp.float32
    )


def core_call(blocks, tokens, width, devices):
    size = 4 * tokens + META
    counts = tuple(b.shape[0] // size for b in blocks)
    total = tokens * devices
    segments = 2 * devices
    vmem = pl.BlockSpec(memory_space=pltpu.VMEM)
    square = jax.ShapeDtypeStruct((tokens, width), jnp.float32)
    import functools

    return pl.pallas_call(
        functools.partial(core_kernel, counts, tokens, width),
        out_shape=(
            jax.ShapeDtypeStruct((tokens, width), jnp.bfloat16),
            square,
            square,
            square,
            jax.ShapeDtypeStruct((1, tokens), jnp.float32),
        ),
        in_specs=[vmem] * len(blocks),
        out_specs=[vmem] * 5,
        scratch_shapes=[pltpu.VMEM((total, width), jnp.bfloat16)] * 4
        + [
            pltpu.VMEM((segments, tokens), jnp.float32),
            pltpu.VMEM((1, total), jnp.float32),
            pltpu.VMEM((2, ROWS, total), jnp.float32),
            pltpu.VMEM((2, ROWS, total), jnp.float32),
            pltpu.VMEM((tokens, total), jnp.float32),
            pltpu.VMEM((tokens, total), jnp.float32),
            pltpu.VMEM((total, width), jnp.float32),
            pltpu.VMEM((total, width), jnp.float32),
            pltpu.VMEM((total, width), jnp.float32),
            pltpu.VMEM((8, total), jnp.float32),
            pltpu.VMEM((segments // 2, tokens), jnp.float32),
        ],
        compiler_params=pltpu.CompilerParams(vmem_limit_bytes=40 * 2**20),
        name="core",
    )(*blocks)


def shift(x, devices, ring=0, flip=0):
    line = devices // 4
    pairs = []
    for i in range(devices):
        place, low = i // 4, i % 4
        pairs.append((i, ((place + ring) % line) * 4 + (low ^ flip)))
    return lax.ppermute(x, "seq", pairs)


def gather_blocks(x, devices):
    a = shift(x, devices, flip=2)
    b = shift(x, devices, ring=1)
    c = shift(x, devices, ring=-1)
    d = shift(c, devices, flip=2)
    e = shift(a, devices, ring=1)
    f = shift(c, devices, ring=-1)
    g = shift(f, devices, flip=2)
    near = [x, a, b, c, d, e, f, g]
    return near + [shift(t, devices, flip=1) for t in near]


def local_small(queries, keys, values, log_gate, out_grad, segment_order):
    tokens, width = queries.shape
    devices = lax.axis_size("seq")
    vmem = pl.BlockSpec(memory_space=pltpu.VMEM)
    packed = pl.pallas_call(
        pack_kernel,
        out_shape=jax.ShapeDtypeStruct((4 * tokens + META, width), jnp.bfloat16),
        in_specs=[pl.BlockSpec(memory_space=pltpu.HBM)] * 6,
        out_specs=vmem,
        scratch_shapes=[
            pltpu.VMEM((1, tokens), jnp.float32),
            pltpu.VMEM((1, 2), jnp.int32),
            pltpu.SemaphoreType.DMA((6,)),
        ],
        compiler_params=pltpu.CompilerParams(vmem_limit_bytes=2 * 2**20),
        name="pack",
    )(*[pltpu.with_memory_space_constraint(t, pltpu.HBM) for t in (queries, keys, values, out_grad, log_gate.reshape(1, tokens), segment_order.reshape(1, 2))])
    blocks = gather_blocks(packed, devices)
    out, dq, dk, dv, gate = core_call(blocks, tokens, width, devices)
    return (out, dq, dk, dv, gate.reshape(tokens))


def local(queries, keys, values, log_gate, out_grad, segment_order):
    tokens, width = queries.shape
    small = tokens == 128 and width == 128 and lax.axis_size("seq") == 16
    path = local_small if small else local_general
    return path(queries, keys, values, log_gate, out_grad, segment_order)


def solution(mesh):
    placed = (
        P(("grp", "seq"), None),
        P(("grp", "seq"), None),
        P(("grp", "seq"), None),
        P(("grp", "seq")),
        P(("grp", "seq"), None),
        P(("grp", "seq")),
    )
    return jax.shard_map(
        local,
        mesh=mesh,
        in_specs=placed,
        out_specs=(
            P(("grp", "seq"), None),
            P(("grp", "seq"), None),
            P(("grp", "seq"), None),
            P(("grp", "seq"), None),
            P(("grp", "seq")),
        ),
        check_vma=False,
    )
```

```python
import functools

import jax
import jax.numpy as jnp
from jax import lax
from jax.experimental import pallas as pl
from jax.experimental.pallas import tpu as pltpu
from jax.sharding import PartitionSpec as P


masked_value = -1e30


def contract_last(left, right):
    return lax.dot_general(
        left, right, (((1,), (1,)), ((), ())), preferred_element_type=jnp.float32
    )


def contract_first(left, right):
    return lax.dot_general(
        left, right, (((0,), (0,)), ((), ())), preferred_element_type=jnp.float32
    )


def tile_scores(query_rows, query_gate, query_pos, key_rows, key_gate, key_pos, score_scale):
    scores = (
        contract_last(query_rows, key_rows) * score_scale + query_gate[:, None] - key_gate[None, :]
    )
    visible = key_pos[None, :] <= query_pos[:, None]
    return (scores, visible)


def tile_probs(scores, visible, row_total):
    return jnp.where(visible, jnp.exp(scores - row_total[:, None]), 0.0)


def local_general(queries, keys, values, log_gate, out_grad, segment_order):
    tokens_here, width = queries.shape
    devices = lax.axis_size("seq")
    segment_rows = tokens_here // 2
    total_len = tokens_here * devices
    score_scale = width ** (-0.5)
    offsets_in = lax.broadcasted_iota(jnp.int32, (1, segment_rows), 1)
    local_cum = jnp.cumsum(log_gate.reshape(2, segment_rows), axis=1)
    segment_total = local_cum[:, -1]
    segment_place = segment_order.astype(jnp.float32)
    own_pos = (segment_order[:, None] * segment_rows + offsets_in).reshape(-1)
    all_totals, all_place = (
        lax.all_gather(segment_total, "seq", axis=0, tiled=True),
        lax.all_gather(segment_place, "seq", axis=0, tiled=True),
    )
    earlier = (all_place[None, :] < segment_place[:, None]).astype(jnp.float32)
    own_offset = jnp.sum(earlier * all_totals[None, :], axis=1)
    own_gate = (local_cum + own_offset[:, None]).reshape(-1)
    all_gate = lax.all_gather(own_gate, "seq", axis=0, tiled=True)
    all_pos = (all_place.astype(jnp.int32)[:, None] * segment_rows + offsets_in).reshape(-1)
    key_all, value_all = (
        lax.all_gather(keys, "seq", axis=0, tiled=True),
        lax.all_gather(values, "seq", axis=0, tiled=True),
    )
    block = 2048
    count = total_len // block

    def key_tile(block_index):
        start = block_index * block
        return (
            lax.dynamic_slice_in_dim(key_all, start, block),
            lax.dynamic_slice_in_dim(value_all, start, block),
            lax.dynamic_slice_in_dim(all_gate, start, block),
            lax.dynamic_slice_in_dim(all_pos, start, block),
        )

    def stats_step(block_index, carry):
        run_max, run_sum = carry
        key_rows, _, key_gate, key_pos = key_tile(block_index)
        scores, visible = tile_scores(
            queries, own_gate, own_pos, key_rows, key_gate, key_pos, score_scale
        )
        kept = jnp.where(visible, scores, masked_value)
        new_max = jnp.maximum(run_max, jnp.max(kept, axis=1))
        fresh = jnp.sum(jnp.where(visible, jnp.exp(kept - new_max[:, None]), 0.0), axis=1)
        return (new_max, run_sum * jnp.exp(run_max - new_max) + fresh)

    start_max = jnp.full((tokens_here,), masked_value, jnp.float32)
    run_max, run_sum = lax.fori_loop(
        0, count, stats_step, (start_max, jnp.zeros((tokens_here,), jnp.float32))
    )
    log_total = run_max + jnp.log(run_sum)

    def output_step(block_index, total):
        key_rows, value_rows, key_gate, key_pos = key_tile(block_index)
        scores, visible = tile_scores(
            queries, own_gate, own_pos, key_rows, key_gate, key_pos, score_scale
        )
        probs = tile_probs(scores, visible, log_total).astype(jnp.bfloat16)
        return total + jnp.dot(probs, value_rows, preferred_element_type=jnp.float32)

    out_full = lax.fori_loop(0, count, output_step, jnp.zeros((tokens_here, width), jnp.float32))
    attn_out = out_full.astype(jnp.bfloat16)
    row_delta = jnp.sum(out_grad.astype(jnp.float32) * out_full, axis=1)

    def row_terms(block_index):
        key_rows, value_rows, key_gate, key_pos = key_tile(block_index)
        scores, visible = tile_scores(
            queries, own_gate, own_pos, key_rows, key_gate, key_pos, score_scale
        )
        probs = tile_probs(scores, visible, log_total)
        dprob = contract_last(out_grad, value_rows)
        return (key_rows, probs, probs * (dprob - row_delta[:, None]))

    def query_step(block_index, total):
        key_rows, _, dscore = row_terms(block_index)
        return total + jnp.dot(
            dscore.astype(jnp.bfloat16), key_rows, preferred_element_type=jnp.float32
        )

    query_acc = lax.fori_loop(0, count, query_step, jnp.zeros((tokens_here, width), jnp.float32))
    query_all, grad_all = (
        lax.all_gather(queries, "seq", axis=0, tiled=True),
        lax.all_gather(out_grad, "seq", axis=0, tiled=True),
    )
    total_all, delta_all = (
        lax.all_gather(log_total, "seq", axis=0, tiled=True),
        lax.all_gather(row_delta, "seq", axis=0, tiled=True),
    )

    def column_step(block_index, carry):
        key_acc, value_acc, column_acc = carry
        start = block_index * block
        query_rows = lax.dynamic_slice_in_dim(query_all, start, block)
        grad_rows = lax.dynamic_slice_in_dim(grad_all, start, block)
        scores, visible = tile_scores(
            query_rows,
            lax.dynamic_slice_in_dim(all_gate, start, block),
            lax.dynamic_slice_in_dim(all_pos, start, block),
            keys,
            own_gate,
            own_pos,
            score_scale,
        )
        probs = tile_probs(scores, visible, lax.dynamic_slice_in_dim(total_all, start, block))
        dprob = contract_last(grad_rows, values)
        dscore = probs * (dprob - lax.dynamic_slice_in_dim(delta_all, start, block)[:, None])
        dscore_low = dscore.astype(jnp.bfloat16)
        key_acc = key_acc + contract_first(dscore_low, query_rows) * score_scale
        value_acc = value_acc + contract_first(probs.astype(jnp.bfloat16), grad_rows)
        column_acc = column_acc - jnp.sum(dscore, axis=0)
        return (key_acc, value_acc, column_acc)

    zeros_own = jnp.zeros((tokens_here, width), jnp.float32)
    key_grad, value_grad, gate_point = lax.fori_loop(
        0, count, column_step, (zeros_own, zeros_own, jnp.zeros((tokens_here,), jnp.float32))
    )
    query_grad = query_acc * score_scale
    point_rows = gate_point.reshape(2, segment_rows)
    within = jnp.flip(jnp.cumsum(jnp.flip(point_rows, 1), axis=1), 1)
    all_point = lax.all_gather(within[:, 0], "seq", axis=0, tiled=True)
    later = (all_place[None, :] > segment_place[:, None]).astype(jnp.float32)
    gate_grad = (within + jnp.sum(later * all_point[None, :], axis=1)[:, None]).reshape(-1)
    return (attn_out, query_grad, key_grad, value_grad, gate_grad)


LOG2E = 1.4426950408889634
META = 16
ROWS = 256
COLS = 256


def pack_kernel(q_ref, k_ref, v_ref, g_ref, gate_hbm, order_hbm, out_ref, gate_ref, order_ref, sems):
    tokens = q_ref.shape[0]
    copies = [
        pltpu.make_async_copy(gate_hbm, gate_ref, sems.at[0]),
        pltpu.make_async_copy(order_hbm, order_ref, sems.at[1]),
    ]
    for index, ref in enumerate((q_ref, k_ref, v_ref, g_ref)):
        copies.append(
            pltpu.make_async_copy(
                ref, out_ref.at[pl.ds(index * tokens, tokens), :], sems.at[index + 2]
            )
        )
    for copy in copies:
        copy.start()
    copies[0].wait()
    copies[1].wait()
    gate = gate_ref[...]
    high = gate.astype(jnp.bfloat16).astype(jnp.float32)
    rest = gate - high
    mid = rest.astype(jnp.bfloat16).astype(jnp.float32)
    low = rest - mid
    lane = lax.broadcasted_iota(jnp.int32, (META, tokens), 1)
    row = lax.broadcasted_iota(jnp.int32, (META, tokens), 0)
    order = order_ref[...].astype(jnp.float32)
    place = jnp.where(lane < tokens // 2, order[:, 0:1], order[:, 1:2])
    meta = jnp.where(
        row == 0, high, jnp.where(row == 1, mid, jnp.where(row == 2, low, place))
    )
    out_ref[4 * tokens : 4 * tokens + META] = meta.astype(jnp.bfloat16)
    for copy in copies[2:]:
        copy.wait()


def split(items, turn, turns):
    return items[len(items) * turn // turns : len(items) * (turn + 1) // turns]


def roll_sum_lanes(x, span, reverse):
    lanes = x.shape[1]
    lane = lax.broadcasted_iota(jnp.int32, x.shape, 1)
    step = 1
    while step < span:
        if reverse:
            x = x + jnp.where(lane < lanes - step, pltpu.roll(x, lanes - step, 1), 0.0)
        else:
            x = x + jnp.where(lane >= step, pltpu.roll(x, step, 1), 0.0)
        step *= 2
    return x


def roll_sum_rows(x, reverse):
    rows = x.shape[0]
    row = lax.broadcasted_iota(jnp.int32, x.shape, 0)
    step = 1
    while step < rows:
        if reverse:
            x = x + jnp.where(row < rows - step, pltpu.roll(x, rows - step, 0), 0.0)
        else:
            x = x + jnp.where(row >= step, pltpu.roll(x, step, 0), 0.0)
        step *= 2
    return x


def core_kernel(counts, tokens, width, *refs):
    blocks = refs[: len(counts)]
    out_ref, dq_ref, dk_ref, dv_ref, gate_ref = refs[len(counts) : len(counts) + 5]
    (qs, ks, vs, gs, cums, key_row, scores, probs, own_scores, own_dprobs, total_col, delta_col,
     outs, points, point_rows) = refs[len(counts) + 5 :]
    seg = tokens // 2
    total = qs.shape[0]
    segments = total // seg
    size = 4 * tokens + META
    scale = width ** (-0.5)
    lane1 = lax.broadcasted_iota(jnp.int32, (1, tokens), 1)
    left = lane1 < seg

    places = []
    for ref, count in zip(blocks, counts):
        for index in range(count):
            base = index * size
            meta = ref[base + 4 * tokens : base + size].astype(jnp.float32)
            gate = (meta[0:1] + meta[1:2]) + meta[2:3]
            place = meta[3:4].astype(jnp.int32)
            pair = (place[0, 0], place[0, seg])
            places.append((ref, base, pair))
            for half in range(2):
                at = pl.multiple_of(pair[half] * seg, seg)
                for slot, dest in enumerate((qs, ks)):
                    first = base + slot * tokens + half * seg
                    dest[pl.ds(at, seg), :] = ref[first : first + seg, :]
                shifted = gate if half == 0 else pltpu.roll(gate, seg, 1)
                cums[pl.ds(pair[half], 1), :] = jnp.where(left, shifted, 0.0)
    own_place = places[0][2]

    inside = roll_sum_lanes(cums[...], seg, False)
    whole = jnp.broadcast_to(inside[:, seg - 1 : seg], inside.shape)
    before = roll_sum_rows(whole, False) - whole
    cums[...] = (inside + before) * LOG2E
    for tile in range(segments // 2):
        even = cums[2 * tile : 2 * tile + 1, :]
        odd = pltpu.roll(cums[2 * tile + 1 : 2 * tile + 2, :], seg, 1)
        key_row[:, tile * tokens : (tile + 1) * tokens] = jnp.where(left, even, odd)

    for ref, base, pair in places:
        for half in range(2):
            at = pl.multiple_of(pair[half] * seg, seg)
            for slot, dest in ((2, vs), (3, gs)):
                first = base + slot * tokens + half * seg
                dest[pl.ds(at, seg), :] = ref[first : first + seg, :]

    points[...] = jnp.zeros_like(points)
    own = blocks[0]
    starts = [pl.multiple_of(p * seg, seg) for p in own_place]
    own_q = own[0:tokens, :]
    own_k = own[tokens : 2 * tokens, :]
    own_v = own[2 * tokens : 3 * tokens, :]
    own_g = own[3 * tokens : 4 * tokens, :]
    key_lines = [cums[pl.ds(p, 1), :] for p in own_place]
    own_key = jnp.where(left, key_lines[0], pltpu.roll(key_lines[1], seg, 1))
    col_pos = jnp.where(left, starts[0] + lane1, starts[1] + lane1 - seg)
    inner = lax.broadcasted_iota(jnp.int32, (tokens, 1), 0)
    row_pos = jnp.where(inner < seg, starts[0] + inner, starts[1] + inner - seg)
    dk_ref[...] = jnp.zeros_like(dk_ref)
    dv_ref[...] = jnp.zeros_like(dv_ref)

    size_r, size_c = ROWS, COLS
    blocks_r = total // size_r
    row_in = lax.broadcasted_iota(jnp.int32, (size_r, size_c), 0)
    col_in = lax.broadcasted_iota(jnp.int32, (size_r, size_c), 1)
    causal = [col_in <= row_in + at for at in range(0, max(size_c, size_r), size_r)]
    factor = scale * LOG2E
    best = {}
    slots = {}

    def rows_of(ref, block):
        return ref[block * size_r : (block + 1) * size_r, :]

    def spread(column):
        return jnp.broadcast_to(column, (column.shape[0], width))

    def tiles_of(block):
        return range(((block + 1) * size_r + size_c - 1) // size_c)

    def score_tile(block, tile):
        c0 = tile * size_c
        s = contract_last(rows_of(qs, block), ks[c0 : c0 + size_c, :]) * factor
        s = s - key_row[:, c0 : c0 + size_c]
        if c0 + size_c > block * size_r:
            s = jnp.where(causal[block % len(causal)], s, masked_value)
        scores[slots[block], :, c0 : c0 + size_c] = s
        part = s[:, :width]
        for at in range(width, size_c, width):
            part = jnp.maximum(part, s[:, at : at + width])
        best[block] = jnp.maximum(best[block], part) if block in best else part

    def own_row_tile(tile):
        c0 = tile * size_c
        s = contract_last(own_q, ks[c0 : c0 + size_c, :]) * factor - key_row[:, c0 : c0 + size_c]
        seen = lax.broadcasted_iota(jnp.int32, (tokens, size_c), 1) + c0 <= row_pos
        own_scores[:, c0 : c0 + size_c] = jnp.where(seen, s, masked_value)
        own_dprobs[:, c0 : c0 + size_c] = contract_last(own_g, vs[c0 : c0 + size_c, :])

    def totals(block):
        top = spread(jnp.max(best[block], axis=1, keepdims=True))
        mass = None
        for at in range(0, len(tiles_of(block)) * size_c, width):
            e = jnp.exp2(scores[slots[block], :, at : at + width] - top)
            mass = e if mass is None else mass + e
        total_col[block * size_r : (block + 1) * size_r, :] = top + spread(
            jnp.log2(jnp.sum(mass, axis=1, keepdims=True))
        )

    def prob_tile(block, tile, low):
        log_total = rows_of(total_col, block)
        for at in range(tile * size_c, (tile + 1) * size_c, width):
            p = jnp.exp2(scores[slots[block], :, at : at + width] - log_total)
            probs[slots[block], :, at : at + width] = p
            low.append(p.astype(jnp.bfloat16))

    def outputs(block, low):
        wide = len(tiles_of(block)) * size_c
        acc = jnp.dot(
            jnp.concatenate(low, axis=1), vs[:wide, :], preferred_element_type=jnp.float32
        )
        outs[block * size_r : (block + 1) * size_r, :] = acc
        g = rows_of(gs, block).astype(jnp.float32)
        delta_col[block * size_r : (block + 1) * size_r, :] = spread(
            jnp.sum(g * acc, axis=1, keepdims=True)
        )

    def own_cols(block):
        r0 = block * size_r
        g = rows_of(gs, block)
        s = contract_last(rows_of(qs, block), own_k) * factor - own_key
        seen = lax.broadcasted_iota(jnp.int32, (size_r, tokens), 0) + r0 >= col_pos
        p = jnp.where(seen, jnp.exp2(s - rows_of(total_col, block)), 0.0)
        ds = p * (contract_last(g, own_v) - rows_of(delta_col, block))
        dv_ref[...] += contract_first(p.astype(jnp.bfloat16), g)
        dk_ref[...] += contract_first(ds.astype(jnp.bfloat16), rows_of(qs, block))

    def point_tile(block, tile):
        c0 = tile * size_c
        delta = rows_of(delta_col, block)
        dp = contract_last(rows_of(gs, block), vs[c0 : c0 + size_c, :])
        for at in range(0, size_c, width):
            ds = probs[slots[block], :, c0 + at : c0 + at + width] * (dp[:, at : at + width] - delta)
            points[:, c0 + at : c0 + at + width] += jnp.sum(
                ds.reshape(size_r // 8, 8, width), axis=0
            )

    rest = list(range(1, blocks_r))
    sequence = []
    while rest:
        sequence.append(rest.pop(0))
        if rest:
            sequence.append(rest.pop())
    sequence.append(0)
    slots.update({block: step % 2 for step, block in enumerate(sequence)})
    first = sequence[0]
    for tile in tiles_of(first):
        score_tile(first, tile)
    totals(first)
    row_tiles = list(range(total // size_c))
    for step, block in enumerate(sequence):
        after = sequence[step + 1] if step + 1 < blocks_r else None
        ahead = list(tiles_of(after)) if after is not None else []
        here = list(tiles_of(block))
        low = []
        for turn in range(max(len(here), len(ahead))):
            for tile in split(ahead, turn, max(len(here), len(ahead))):
                score_tile(after, tile)
            for tile in split(here, turn, max(len(here), len(ahead))):
                prob_tile(block, tile, low)
        outputs(block, low)
        if after is not None:
            totals(after)
        if row_tiles and step % max(1, blocks_r // (total // size_c)) == 0:
            own_row_tile(row_tiles.pop(0))
        for tile in here:
            point_tile(block, tile)
        own_cols(block)
    dk_ref[...] = dk_ref[...] * scale

    def pick(ref):
        return jnp.concatenate([ref[pl.ds(s, seg), :] for s in starts], axis=0)

    log_total, delta = pick(total_col), pick(delta_col)
    out_ref[...] = pick(outs).astype(jnp.bfloat16)
    low = []
    for at in range(0, total, width):
        p = jnp.exp2(own_scores[:, at : at + width] - log_total)
        ds = p * (own_dprobs[:, at : at + width] - delta)
        low.append(ds.astype(jnp.bfloat16))
    dq_ref[...] = scale * jnp.dot(
        jnp.concatenate(low, axis=1), ks[...], preferred_element_type=jnp.float32
    )

    for tile in range(segments // 2):
        c0 = tile * tokens
        point_rows[tile : tile + 1, :] = -jnp.sum(
            points[:, c0 : c0 + tokens], axis=0, keepdims=True
        )
    inside = roll_sum_lanes(point_rows[...], tokens, True)
    whole = jnp.broadcast_to(inside[:, 0:1], inside.shape)
    point_rows[...] = inside + (roll_sum_rows(whole, True) - whole)
    halves = []
    for half in range(2):
        line = point_rows[pl.ds(own_place[half] // 2, 1), :]
        turned = pltpu.roll(line, seg, 1)
        halves.append(jnp.where(own_place[half] % 2 == half, line, turned))
    gate_ref[...] = jnp.where(left, halves[0], halves[1])


def core_call(blocks, tokens, width, devices):
    size = 4 * tokens + META
    counts = tuple(b.shape[0] // size for b in blocks)
    total = tokens * devices
    segments = 2 * devices
    vmem = pl.BlockSpec(memory_space=pltpu.VMEM)
    square = jax.ShapeDtypeStruct((tokens, width), jnp.float32)
    return pl.pallas_call(
        functools.partial(core_kernel, counts, tokens, width),
        out_shape=(
            jax.ShapeDtypeStruct((tokens, width), jnp.bfloat16),
            square,
            square,
            square,
            jax.ShapeDtypeStruct((1, tokens), jnp.float32),
        ),
        in_specs=[vmem] * len(blocks),
        out_specs=[vmem] * 5,
        scratch_shapes=[pltpu.VMEM((total, width), jnp.bfloat16)] * 4
        + [
            pltpu.VMEM((segments, tokens), jnp.float32),
            pltpu.VMEM((1, total), jnp.float32),
            pltpu.VMEM((2, ROWS, total), jnp.float32),
            pltpu.VMEM((2, ROWS, total), jnp.float32),
            pltpu.VMEM((tokens, total), jnp.float32),
            pltpu.VMEM((tokens, total), jnp.float32),
            pltpu.VMEM((total, width), jnp.float32),
            pltpu.VMEM((total, width), jnp.float32),
            pltpu.VMEM((total, width), jnp.float32),
            pltpu.VMEM((8, total), jnp.float32),
            pltpu.VMEM((segments // 2, tokens), jnp.float32),
        ],
        compiler_params=pltpu.CompilerParams(vmem_limit_bytes=40 * 2**20),
        name="core",
    )(*blocks)


def shift(x, devices, ring=0, flip=0):
    line = devices // 4
    walk = [0] + list(range(1, line, 2)) + list(range(2, line, 2))[::-1]
    pairs = []
    for step, place in enumerate(walk):
        target = walk[(step + ring) % line]
        pairs += [(place * 4 + low, target * 4 + (low ^ flip)) for low in range(4)]
    return lax.ppermute(x, "seq", pairs)


MOVES = (
    ("down", "down", "own"),
    ("up", "up", "own"),
    ("side", "side", "own"),
    ("own_core", "core", "own"),
    ("down_down", "down", "down"),
    ("down_side", "side", "down"),
    ("side_up", "up", "side"),
    ("up_core", "core", "up"),
    ("last", "side", "down_down"),
    ("down_core", "core", "down"),
    ("down_side_core", "core", "down_side"),
    ("side_core", "core", "side"),
    ("side_up_core", "core", "side_up"),
    ("down_down_core", "core", "down_down"),
    ("last_core", "core", "last"),
)
KINDS = {"up": {"ring": 1}, "down": {"ring": -1}, "side": {"flip": 2}, "core": {"flip": 1}}


def gather_blocks(x, devices):
    blocks = {"own": x}
    for name, kind, sent in MOVES:
        blocks[name] = shift(blocks[sent], devices, **KINDS[kind])
    return list(blocks.values())


def local_small(queries, keys, values, log_gate, out_grad, segment_order):
    tokens, width = queries.shape
    devices = lax.axis_size("seq")
    vmem = pl.BlockSpec(memory_space=pltpu.VMEM)
    packed = pl.pallas_call(
        pack_kernel,
        out_shape=jax.ShapeDtypeStruct((4 * tokens + META, width), jnp.bfloat16),
        in_specs=[pl.BlockSpec(memory_space=pltpu.HBM)] * 6,
        out_specs=vmem,
        scratch_shapes=[
            pltpu.VMEM((1, tokens), jnp.float32),
            pltpu.VMEM((1, 2), jnp.int32),
            pltpu.SemaphoreType.DMA((6,)),
        ],
        compiler_params=pltpu.CompilerParams(vmem_limit_bytes=2 * 2**20),
        name="pack",
    )(*[pltpu.with_memory_space_constraint(t, pltpu.HBM) for t in (queries, keys, values, out_grad, log_gate.reshape(1, tokens), segment_order.reshape(1, 2))])
    blocks = gather_blocks(packed, devices)
    out, dq, dk, dv, gate = core_call(blocks, tokens, width, devices)
    return (out, dq, dk, dv, gate.reshape(tokens))


def local(queries, keys, values, log_gate, out_grad, segment_order):
    tokens, width = queries.shape
    small = tokens == 128 and width == 128 and lax.axis_size("seq") == 16
    path = local_small if small else local_general
    return path(queries, keys, values, log_gate, out_grad, segment_order)


def solution(mesh):
    placed = (
        P(("grp", "seq"), None),
        P(("grp", "seq"), None),
        P(("grp", "seq"), None),
        P(("grp", "seq")),
        P(("grp", "seq"), None),
        P(("grp", "seq")),
    )
    return jax.shard_map(
        local,
        mesh=mesh,
        in_specs=placed,
        out_specs=(
            P(("grp", "seq"), None),
            P(("grp", "seq"), None),
            P(("grp", "seq"), None),
            P(("grp", "seq"), None),
            P(("grp", "seq")),
        ),
        check_vma=False,
    )
```

```python
import functools

import jax
import jax.numpy as jnp
from jax import lax
from jax.experimental import pallas as pl
from jax.experimental.pallas import tpu as pltpu
from jax.sharding import PartitionSpec as P


masked_value = -1e30


def contract_last(left, right):
    return lax.dot_general(
        left, right, (((1,), (1,)), ((), ())), preferred_element_type=jnp.float32
    )


def contract_first(left, right):
    return lax.dot_general(
        left, right, (((0,), (0,)), ((), ())), preferred_element_type=jnp.float32
    )


def tile_scores(query_rows, query_gate, query_pos, key_rows, key_gate, key_pos, score_scale):
    scores = (
        contract_last(query_rows, key_rows) * score_scale + query_gate[:, None] - key_gate[None, :]
    )
    visible = key_pos[None, :] <= query_pos[:, None]
    return (scores, visible)


def tile_probs(scores, visible, row_total):
    return jnp.where(visible, jnp.exp(scores - row_total[:, None]), 0.0)


def local_general(queries, keys, values, log_gate, out_grad, segment_order):
    tokens_here, width = queries.shape
    devices = lax.axis_size("seq")
    segment_rows = tokens_here // 2
    total_len = tokens_here * devices
    score_scale = width ** (-0.5)
    offsets_in = lax.broadcasted_iota(jnp.int32, (1, segment_rows), 1)
    local_cum = jnp.cumsum(log_gate.reshape(2, segment_rows), axis=1)
    segment_total = local_cum[:, -1]
    segment_place = segment_order.astype(jnp.float32)
    own_pos = (segment_order[:, None] * segment_rows + offsets_in).reshape(-1)
    all_totals, all_place = (
        lax.all_gather(segment_total, "seq", axis=0, tiled=True),
        lax.all_gather(segment_place, "seq", axis=0, tiled=True),
    )
    earlier = (all_place[None, :] < segment_place[:, None]).astype(jnp.float32)
    own_offset = jnp.sum(earlier * all_totals[None, :], axis=1)
    own_gate = (local_cum + own_offset[:, None]).reshape(-1)
    all_gate = lax.all_gather(own_gate, "seq", axis=0, tiled=True)
    all_pos = (all_place.astype(jnp.int32)[:, None] * segment_rows + offsets_in).reshape(-1)
    key_all, value_all = (
        lax.all_gather(keys, "seq", axis=0, tiled=True),
        lax.all_gather(values, "seq", axis=0, tiled=True),
    )
    block = 2048
    count = total_len // block

    def key_tile(block_index):
        start = block_index * block
        return (
            lax.dynamic_slice_in_dim(key_all, start, block),
            lax.dynamic_slice_in_dim(value_all, start, block),
            lax.dynamic_slice_in_dim(all_gate, start, block),
            lax.dynamic_slice_in_dim(all_pos, start, block),
        )

    def stats_step(block_index, carry):
        run_max, run_sum = carry
        key_rows, _, key_gate, key_pos = key_tile(block_index)
        scores, visible = tile_scores(
            queries, own_gate, own_pos, key_rows, key_gate, key_pos, score_scale
        )
        kept = jnp.where(visible, scores, masked_value)
        new_max = jnp.maximum(run_max, jnp.max(kept, axis=1))
        fresh = jnp.sum(jnp.where(visible, jnp.exp(kept - new_max[:, None]), 0.0), axis=1)
        return (new_max, run_sum * jnp.exp(run_max - new_max) + fresh)

    start_max = jnp.full((tokens_here,), masked_value, jnp.float32)
    run_max, run_sum = lax.fori_loop(
        0, count, stats_step, (start_max, jnp.zeros((tokens_here,), jnp.float32))
    )
    log_total = run_max + jnp.log(run_sum)

    def output_step(block_index, total):
        key_rows, value_rows, key_gate, key_pos = key_tile(block_index)
        scores, visible = tile_scores(
            queries, own_gate, own_pos, key_rows, key_gate, key_pos, score_scale
        )
        probs = tile_probs(scores, visible, log_total).astype(jnp.bfloat16)
        return total + jnp.dot(probs, value_rows, preferred_element_type=jnp.float32)

    out_full = lax.fori_loop(0, count, output_step, jnp.zeros((tokens_here, width), jnp.float32))
    attn_out = out_full.astype(jnp.bfloat16)
    row_delta = jnp.sum(out_grad.astype(jnp.float32) * out_full, axis=1)

    def row_terms(block_index):
        key_rows, value_rows, key_gate, key_pos = key_tile(block_index)
        scores, visible = tile_scores(
            queries, own_gate, own_pos, key_rows, key_gate, key_pos, score_scale
        )
        probs = tile_probs(scores, visible, log_total)
        dprob = contract_last(out_grad, value_rows)
        return (key_rows, probs, probs * (dprob - row_delta[:, None]))

    def query_step(block_index, total):
        key_rows, _, dscore = row_terms(block_index)
        return total + jnp.dot(
            dscore.astype(jnp.bfloat16), key_rows, preferred_element_type=jnp.float32
        )

    query_acc = lax.fori_loop(0, count, query_step, jnp.zeros((tokens_here, width), jnp.float32))
    query_all, grad_all = (
        lax.all_gather(queries, "seq", axis=0, tiled=True),
        lax.all_gather(out_grad, "seq", axis=0, tiled=True),
    )
    total_all, delta_all = (
        lax.all_gather(log_total, "seq", axis=0, tiled=True),
        lax.all_gather(row_delta, "seq", axis=0, tiled=True),
    )

    def column_step(block_index, carry):
        key_acc, value_acc, column_acc = carry
        start = block_index * block
        query_rows = lax.dynamic_slice_in_dim(query_all, start, block)
        grad_rows = lax.dynamic_slice_in_dim(grad_all, start, block)
        scores, visible = tile_scores(
            query_rows,
            lax.dynamic_slice_in_dim(all_gate, start, block),
            lax.dynamic_slice_in_dim(all_pos, start, block),
            keys,
            own_gate,
            own_pos,
            score_scale,
        )
        probs = tile_probs(scores, visible, lax.dynamic_slice_in_dim(total_all, start, block))
        dprob = contract_last(grad_rows, values)
        dscore = probs * (dprob - lax.dynamic_slice_in_dim(delta_all, start, block)[:, None])
        dscore_low = dscore.astype(jnp.bfloat16)
        key_acc = key_acc + contract_first(dscore_low, query_rows) * score_scale
        value_acc = value_acc + contract_first(probs.astype(jnp.bfloat16), grad_rows)
        column_acc = column_acc - jnp.sum(dscore, axis=0)
        return (key_acc, value_acc, column_acc)

    zeros_own = jnp.zeros((tokens_here, width), jnp.float32)
    key_grad, value_grad, gate_point = lax.fori_loop(
        0, count, column_step, (zeros_own, zeros_own, jnp.zeros((tokens_here,), jnp.float32))
    )
    query_grad = query_acc * score_scale
    point_rows = gate_point.reshape(2, segment_rows)
    within = jnp.flip(jnp.cumsum(jnp.flip(point_rows, 1), axis=1), 1)
    all_point = lax.all_gather(within[:, 0], "seq", axis=0, tiled=True)
    later = (all_place[None, :] > segment_place[:, None]).astype(jnp.float32)
    gate_grad = (within + jnp.sum(later * all_point[None, :], axis=1)[:, None]).reshape(-1)
    return (attn_out, query_grad, key_grad, value_grad, gate_grad)


LOG2E = 1.4426950408889634
META = 16


def pack_kernel(q_ref, k_ref, v_ref, g_ref, gate_hbm, order_hbm, out_ref, gate_ref, order_ref, sems):
    tokens = q_ref.shape[0]
    copies = [
        pltpu.make_async_copy(gate_hbm, gate_ref, sems.at[0]),
        pltpu.make_async_copy(order_hbm, order_ref, sems.at[1]),
    ]
    for index, ref in enumerate((q_ref, k_ref, v_ref, g_ref)):
        copies.append(
            pltpu.make_async_copy(
                ref, out_ref.at[pl.ds(index * tokens, tokens), :], sems.at[index + 2]
            )
        )
    for copy in copies:
        copy.start()
    copies[0].wait()
    copies[1].wait()
    gate = gate_ref[...]
    high = gate.astype(jnp.bfloat16).astype(jnp.float32)
    rest = gate - high
    mid = rest.astype(jnp.bfloat16).astype(jnp.float32)
    low = rest - mid
    lane = lax.broadcasted_iota(jnp.int32, (META, tokens), 1)
    row = lax.broadcasted_iota(jnp.int32, (META, tokens), 0)
    order = order_ref[...].astype(jnp.float32)
    place = jnp.where(lane < tokens // 2, order[:, 0:1], order[:, 1:2])
    meta = jnp.where(
        row == 0, high, jnp.where(row == 1, mid, jnp.where(row == 2, low, place))
    )
    out_ref[4 * tokens : 4 * tokens + META] = meta.astype(jnp.bfloat16)
    for copy in copies[2:]:
        copy.wait()


def split(items, turn, turns):
    return items[len(items) * turn // turns : len(items) * (turn + 1) // turns]


def block_order(steps):
    return [1] + list(range(steps - 1, 1, -1)) + [0]


def roll_sum_lanes(x, span, reverse):
    lanes = x.shape[1]
    lane = lax.broadcasted_iota(jnp.int32, x.shape, 1)
    step = 1
    while step < span:
        if reverse:
            x = x + jnp.where(lane < lanes - step, pltpu.roll(x, lanes - step, 1), 0.0)
        else:
            x = x + jnp.where(lane >= step, pltpu.roll(x, step, 1), 0.0)
        step *= 2
    return x


def roll_sum_rows(x, reverse):
    rows = x.shape[0]
    row = lax.broadcasted_iota(jnp.int32, x.shape, 0)
    step = 1
    while step < rows:
        if reverse:
            x = x + jnp.where(row < rows - step, pltpu.roll(x, rows - step, 0), 0.0)
        else:
            x = x + jnp.where(row >= step, pltpu.roll(x, step, 0), 0.0)
        step *= 2
    return x


def spread(column, width):
    return jnp.broadcast_to(column, (column.shape[0], width))


def halves(x, width):
    return [x[:, at : at + width] for at in range(0, x.shape[1], width)]


def log_total_of(pieces, width):
    best = pieces[0]
    for s in pieces[1:]:
        best = jnp.maximum(best, s)
    top = spread(jnp.max(best, axis=1, keepdims=True), width)
    mass = jnp.exp2(pieces[0] - top)
    for s in pieces[1:]:
        mass = mass + jnp.exp2(s - top)
    return top + spread(jnp.log2(jnp.sum(mass, axis=1, keepdims=True)), width)


def score_of(q, ks, key_row, tile, cols, factor):
    c0 = tile * cols
    return contract_last(q, ks[c0 : c0 + cols, :]) * factor - key_row[:, c0 : c0 + cols]


def start_rows(own, place, ks, key_row, own_s, own_total):
    total, width = ks.shape
    tokens = own_s.shape[0]
    seg = tokens // 2
    cols = 2 * tokens
    inner = lax.broadcasted_iota(jnp.int32, (tokens, 1), 0)
    row_pos = jnp.where(inner < seg, place[0] * seg + inner, place[1] * seg + inner - seg)
    q = own[0:tokens, :]
    pieces = []
    for tile in range(total // cols):
        c0 = tile * cols
        seen = lax.broadcasted_iota(jnp.int32, (tokens, cols), 1) + c0 <= row_pos
        s = score_of(q, ks, key_row, tile, cols, width ** (-0.5) * LOG2E)
        s = jnp.where(seen, s, masked_value)
        own_s[:, c0 : c0 + cols] = s
        pieces += halves(s, width)
    own_total[...] = log_total_of(pieces, width)


def row_kernel(own, ks, vs, own_s, own_total, out_ref, dq_ref):
    total, width = ks.shape
    tokens = out_ref.shape[0]
    cols = 2 * tokens
    g = own[3 * tokens : 4 * tokens, :]
    log_total = own_total[...]
    p, dps = [], []
    for tile in range(total // cols):
        c0 = tile * cols
        p += [jnp.exp2(s - log_total) for s in halves(own_s[:, c0 : c0 + cols], width)]
        dps += halves(contract_last(g, vs[c0 : c0 + cols, :]), width)
    low = jnp.concatenate([t.astype(jnp.bfloat16) for t in p], axis=1)
    out = jnp.dot(low, vs[...], preferred_element_type=jnp.float32)
    out_ref[...] = out.astype(jnp.bfloat16)
    delta = spread(jnp.sum(g.astype(jnp.float32) * out, axis=1, keepdims=True), width)
    low = jnp.concatenate(
        [(t * (dp - delta)).astype(jnp.bfloat16) for t, dp in zip(p, dps)], axis=1
    )
    dq_ref[...] = width ** (-0.5) * jnp.dot(low, ks[...], preferred_element_type=jnp.float32)


def core_kernel(counts, partner, tokens, width, core_ref, *refs):
    blocks = refs[: len(counts)]
    keep_ref, send_ref, ks, vs, own_s, own_total = refs[len(counts) : len(counts) + 6]
    qs, gs, cums, key_row, points, lines = refs[len(counts) + 6 :]
    seg = tokens // 2
    total = qs.shape[0]
    segments = total // seg
    size = 4 * tokens + META
    scale = width ** (-0.5)
    factor = scale * LOG2E
    lane1 = lax.broadcasted_iota(jnp.int32, (1, tokens), 1)
    left = lane1 < seg

    places = []
    for ref, count in zip(blocks, counts):
        for index in range(count):
            base = index * size
            meta = ref[base + 4 * tokens : base + size].astype(jnp.float32)
            gate = (meta[0:1] + meta[1:2]) + meta[2:3]
            place = meta[3:4].astype(jnp.int32)
            pair = (place[0, 0], place[0, seg])
            places.append((ref, base, pair))
            for half in range(2):
                at = pl.multiple_of(pair[half] * seg, seg)
                for slot, dest in enumerate((qs, ks)):
                    first = base + slot * tokens + half * seg
                    dest[pl.ds(at, seg), :] = ref[first : first + seg, :]
                shifted = gate if half == 0 else pltpu.roll(gate, seg, 1)
                cums[pl.ds(pair[half], 1), :] = jnp.where(left, shifted, 0.0)
    own_place = places[0][2]

    inside = roll_sum_lanes(cums[...], seg, False)
    whole = jnp.broadcast_to(inside[:, seg - 1 : seg], inside.shape)
    before = roll_sum_rows(whole, False) - whole
    cums[...] = (inside + before) * LOG2E
    for tile in range(segments // 2):
        even = cums[2 * tile : 2 * tile + 1, :]
        odd = pltpu.roll(cums[2 * tile + 1 : 2 * tile + 2, :], seg, 1)
        key_row[:, tile * tokens : (tile + 1) * tokens] = jnp.where(left, even, odd)

    for ref, base, pair in places:
        for half in range(2):
            at = pl.multiple_of(pair[half] * seg, seg)
            for slot, dest in ((2, vs), (3, gs)):
                first = base + slot * tokens + half * seg
                dest[pl.ds(at, seg), :] = ref[first : first + seg, :]

    points[...] = jnp.zeros_like(points)
    inner = lax.broadcasted_iota(jnp.int32, (tokens, 1), 0)
    own = blocks[0]

    other = blocks[partner]
    pair_k = jnp.concatenate([own[tokens : 2 * tokens, :], other[tokens : 2 * tokens, :]], axis=0)
    pair_v = jnp.concatenate(
        [own[2 * tokens : 3 * tokens, :], other[2 * tokens : 3 * tokens, :]], axis=0
    )
    firsts = [0, sum(counts[:partner])]
    pair_key, pair_pos = [], []
    for first in firsts:
        place = places[first][2]
        key = [cums[pl.ds(p, 1), :] for p in place]
        pair_key.append(jnp.where(left, key[0], pltpu.roll(key[1], seg, 1)))
        pair_pos.append(
            jnp.where(left, place[0] * seg + lane1, place[1] * seg + lane1 - seg)
        )
    pair_key = jnp.concatenate(pair_key, axis=1)
    pair_pos = jnp.concatenate(pair_pos, axis=1)

    rows, cols = tokens, 2 * tokens
    steps = total // cols
    core = core_ref[0, 0]
    row_in = lax.broadcasted_iota(jnp.int32, (rows, cols), 0) + core * rows
    col_in = lax.broadcasted_iota(jnp.int32, (rows, cols), 1)
    causal = col_in <= row_in
    state = {}

    def open_item(item):
        r0 = pl.multiple_of((2 * item + core) * rows, rows)
        state[item] = dict(
            q=qs[pl.ds(r0, rows), :], g=gs[pl.ds(r0, rows), :], r0=r0, tiles=item + 1,
            s=[], p=[], low=[],
        )

    def score_tile(item, tile):
        it = state[item]
        s = score_of(it["q"], ks, key_row, tile, cols, factor)
        if tile == item:
            s = jnp.where(causal, s, masked_value)
        it["s"] += halves(s, width)

    def prob_tile(item, tile):
        it = state[item]
        for s in it["s"][2 * tile : 2 * tile + 2]:
            p = jnp.exp2(s - it["total"])
            it["p"].append(p)
            it["low"].append(p.astype(jnp.bfloat16))

    def outputs(item):
        it = state[item]
        out = jnp.dot(
            jnp.concatenate(it["low"], axis=1),
            vs[: it["tiles"] * cols, :],
            preferred_element_type=jnp.float32,
        )
        g = it["g"].astype(jnp.float32)
        it["delta"] = spread(jnp.sum(g * out, axis=1, keepdims=True), width)

    sums = dict(k=jnp.zeros((cols, width), jnp.float32), v=jnp.zeros((cols, width), jnp.float32))

    def pair_columns(item):
        it = state[item]
        s = contract_last(it["q"], pair_k) * factor - pair_key
        seen = pair_pos <= it["r0"] + inner
        p = jnp.where(seen, jnp.exp2(s - jnp.concatenate([it["total"]] * 2, axis=1)), 0.0)
        ds = p * (contract_last(it["g"], pair_v) - jnp.concatenate([it["delta"]] * 2, axis=1))
        sums["v"] = sums["v"] + contract_first(p.astype(jnp.bfloat16), it["g"])
        sums["k"] = sums["k"] + contract_first(ds.astype(jnp.bfloat16), it["q"])

    def last_stage(item):
        it = state[item]
        for tile in range(it["tiles"]):
            c0 = tile * cols
            dp = halves(contract_last(it["g"], vs[c0 : c0 + cols, :]), width)
            for at in range(2):
                ds = it["p"][2 * tile + at] * (dp[at] - it["delta"])
                first = c0 + at * width
                points[:, first : first + width] += jnp.sum(
                    ds.reshape(rows // 8, 8, width), axis=0
                )
        pair_columns(item)

    order = block_order(steps)
    open_item(order[0])
    for tile in range(state[order[0]]["tiles"]):
        score_tile(order[0], tile)
    state[order[0]]["total"] = log_total_of(state[order[0]]["s"], width)
    for turn, item in enumerate(order):
        after = order[turn + 1] if turn + 1 < len(order) else None
        here = list(range(state[item]["tiles"]))
        ahead = []
        if after is not None:
            open_item(after)
            ahead = list(range(state[after]["tiles"]))
        count = max(len(here), len(ahead))
        for at in range(count):
            for tile in split(ahead, at, count):
                score_tile(after, tile)
            for tile in split(here, at, count):
                prob_tile(item, tile)
        outputs(item)
        if after is not None:
            state[after]["total"] = log_total_of(state[after]["s"], width)
        last_stage(item)

    for tile in range(total // width):
        lines[tile : tile + 1, :] = -jnp.sum(
            points[:, tile * width : (tile + 1) * width], axis=0, keepdims=True
        )
    inside = roll_sum_lanes(lines[...], tokens, True)
    whole = jnp.broadcast_to(inside[:, 0:1], inside.shape)
    lines[...] = inside + (roll_sum_rows(whole, True) - whole)
    for index, ref in enumerate((keep_ref, send_ref)):
        ref[0:tokens, :] = sums["k"][index * tokens : (index + 1) * tokens, :] * scale
        ref[tokens : 2 * tokens, :] = sums["v"][index * tokens : (index + 1) * tokens, :]
        parts = []
        for half, place in enumerate(places[firsts[index]][2]):
            line = lines[pl.ds(place // 2, 1), :]
            parts.append(jnp.where(place % 2 == half, line, pltpu.roll(line, seg, 1)))
        ref[2 * tokens : 2 * tokens + 8, :] = jnp.broadcast_to(
            jnp.where(left, parts[0], parts[1]), (8, width)
        )
    start_rows(own, own_place, ks, key_row, own_s, own_total)


def join_kernel(keep_ref, got_ref, dk_ref, dv_ref, gate_ref):
    tokens = dk_ref.shape[0]
    dk_ref[...] = keep_ref[0:tokens, :] + got_ref[0:tokens, :]
    dv_ref[...] = keep_ref[tokens : 2 * tokens, :] + got_ref[tokens : 2 * tokens, :]
    gate_ref[...] = keep_ref[2 * tokens : 2 * tokens + 1, :] + got_ref[2 * tokens : 2 * tokens + 1, :]


def core_call(blocks, tokens, width, devices, core, partner):
    size = 4 * tokens + META
    counts = tuple(b.shape[0] // size for b in blocks)
    total = tokens * devices
    segments = 2 * devices
    vmem = pl.BlockSpec(memory_space=pltpu.VMEM)
    smem = pl.BlockSpec(memory_space=pltpu.SMEM)
    part = jax.ShapeDtypeStruct((2 * tokens + 8, width), jnp.float32)
    sorted_rows = jax.ShapeDtypeStruct((total, width), jnp.bfloat16)
    return pl.pallas_call(
        functools.partial(core_kernel, counts, partner, tokens, width),
        out_shape=(
            part,
            part,
            sorted_rows,
            sorted_rows,
            jax.ShapeDtypeStruct((tokens, total), jnp.float32),
            jax.ShapeDtypeStruct((tokens, width), jnp.float32),
        ),
        in_specs=[smem] + [vmem] * len(blocks),
        out_specs=[vmem] * 6,
        scratch_shapes=[
            pltpu.VMEM((total, width), jnp.bfloat16),
            pltpu.VMEM((total, width), jnp.bfloat16),
            pltpu.VMEM((segments, tokens), jnp.float32),
            pltpu.VMEM((1, total), jnp.float32),
            pltpu.VMEM((8, total), jnp.float32),
            pltpu.VMEM((total // width, width), jnp.float32),
        ],
        compiler_params=pltpu.CompilerParams(vmem_limit_bytes=40 * 2**20),
        name="core",
    )(core, *blocks)


def row_call(own, ks, vs, own_s, own_total, tokens, width):
    vmem = pl.BlockSpec(memory_space=pltpu.VMEM)
    return pl.pallas_call(
        row_kernel,
        out_shape=(
            jax.ShapeDtypeStruct((tokens, width), jnp.bfloat16),
            jax.ShapeDtypeStruct((tokens, width), jnp.float32),
        ),
        in_specs=[vmem] * 5,
        out_specs=[vmem] * 2,
        compiler_params=pltpu.CompilerParams(vmem_limit_bytes=24 * 2**20),
        cost_estimate=pl.CostEstimate(
            flops=6 * tokens * ks.shape[0] * width,
            bytes_accessed=4 * ks.shape[0] * width,
            transcendentals=tokens * ks.shape[0],
        ),
        name="rows",
    )(own, ks, vs, own_s, own_total)


def join_call(keep, got, tokens, width):
    vmem = pl.BlockSpec(memory_space=pltpu.VMEM)
    square = jax.ShapeDtypeStruct((tokens, width), jnp.float32)
    return pl.pallas_call(
        join_kernel,
        out_shape=(square, square, jax.ShapeDtypeStruct((1, width), jnp.float32)),
        in_specs=[vmem, vmem],
        out_specs=[vmem] * 3,
        compiler_params=pltpu.CompilerParams(vmem_limit_bytes=2 * 2**20),
        name="join",
    )(keep, got)


def shift(x, devices, ring=0, flip=0):
    line = devices // 4
    walk = [0] + list(range(1, line, 2)) + list(range(2, line, 2))[::-1]
    pairs = []
    for step, place in enumerate(walk):
        target = walk[(step + ring) % line]
        pairs += [(place * 4 + low, target * 4 + (low ^ flip)) for low in range(4)]
    return lax.ppermute(x, "seq", pairs)


MOVES = (
    ("down", "down", "own"),
    ("up", "up", "own"),
    ("side", "side", "own"),
    ("own_core", "core", "own"),
    ("down_down", "down", "down"),
    ("down_side", "side", "down"),
    ("side_up", "up", "side"),
    ("up_core", "core", "up"),
    ("last", "side", "down_down"),
    ("down_core", "core", "down"),
    ("down_side_core", "core", "down_side"),
    ("side_core", "core", "side"),
    ("side_up_core", "core", "side_up"),
    ("down_down_core", "core", "down_down"),
    ("last_core", "core", "last"),
)
KINDS = {"up": {"ring": 1}, "down": {"ring": -1}, "side": {"flip": 2}, "core": {"flip": 1}}


def gather_blocks(x, devices):
    blocks = {"own": x}
    for name, kind, sent in MOVES:
        blocks[name] = shift(blocks[sent], devices, **KINDS[kind])
    return list(blocks.values())


def local_small(queries, keys, values, log_gate, out_grad, segment_order):
    tokens, width = queries.shape
    devices = lax.axis_size("seq")
    vmem = pl.BlockSpec(memory_space=pltpu.VMEM)
    packed = pl.pallas_call(
        pack_kernel,
        out_shape=jax.ShapeDtypeStruct((4 * tokens + META, width), jnp.bfloat16),
        in_specs=[pl.BlockSpec(memory_space=pltpu.HBM)] * 6,
        out_specs=vmem,
        scratch_shapes=[
            pltpu.VMEM((1, tokens), jnp.float32),
            pltpu.VMEM((1, 2), jnp.int32),
            pltpu.SemaphoreType.DMA((6,)),
        ],
        compiler_params=pltpu.CompilerParams(vmem_limit_bytes=2 * 2**20),
        name="pack",
    )(*[pltpu.with_memory_space_constraint(t, pltpu.HBM) for t in (queries, keys, values, out_grad, log_gate.reshape(1, tokens), segment_order.reshape(1, 2))])
    blocks = gather_blocks(packed, devices)
    core = (lax.axis_index("seq") % 2).astype(jnp.int32).reshape(1, 1)
    partner = 1 + [m[0] for m in MOVES].index("own_core")
    keep, send, ks, vs, own_s, own_total = core_call(blocks, tokens, width, devices, core, partner)
    got = shift(send, devices, flip=1)
    out, dq = row_call(packed, ks, vs, own_s, own_total, tokens, width)
    dk, dv, gate = join_call(keep, got, tokens, width)
    return (out, dq, dk, dv, gate.reshape(tokens))


def local(queries, keys, values, log_gate, out_grad, segment_order):
    tokens, width = queries.shape
    small = tokens == 128 and width == 128 and lax.axis_size("seq") == 16
    path = local_small if small else local_general
    return path(queries, keys, values, log_gate, out_grad, segment_order)


def solution(mesh):
    placed = (
        P(("grp", "seq"), None),
        P(("grp", "seq"), None),
        P(("grp", "seq"), None),
        P(("grp", "seq")),
        P(("grp", "seq"), None),
        P(("grp", "seq")),
    )
    return jax.shard_map(
        local,
        mesh=mesh,
        in_specs=placed,
        out_specs=(
            P(("grp", "seq"), None),
            P(("grp", "seq"), None),
            P(("grp", "seq"), None),
            P(("grp", "seq"), None),
            P(("grp", "seq")),
        ),
        check_vma=False,
    )
```

```python
import functools

import jax
import jax.numpy as jnp
from jax import lax
from jax.experimental import pallas as pl
from jax.experimental.pallas import tpu as pltpu
from jax.sharding import PartitionSpec as P


masked_value = -1e30


def contract_last(left, right):
    return lax.dot_general(
        left, right, (((1,), (1,)), ((), ())), preferred_element_type=jnp.float32
    )


def contract_first(left, right):
    return lax.dot_general(
        left, right, (((0,), (0,)), ((), ())), preferred_element_type=jnp.float32
    )


def tile_scores(query_rows, query_gate, query_pos, key_rows, key_gate, key_pos, score_scale):
    scores = (
        contract_last(query_rows, key_rows) * score_scale + query_gate[:, None] - key_gate[None, :]
    )
    visible = key_pos[None, :] <= query_pos[:, None]
    return (scores, visible)


def tile_probs(scores, visible, row_total):
    return jnp.where(visible, jnp.exp(scores - row_total[:, None]), 0.0)


def local_general(queries, keys, values, log_gate, out_grad, segment_order):
    tokens_here, width = queries.shape
    devices = lax.axis_size("seq")
    segment_rows = tokens_here // 2
    total_len = tokens_here * devices
    score_scale = width ** (-0.5)
    offsets_in = lax.broadcasted_iota(jnp.int32, (1, segment_rows), 1)
    local_cum = jnp.cumsum(log_gate.reshape(2, segment_rows), axis=1)
    segment_total = local_cum[:, -1]
    segment_place = segment_order.astype(jnp.float32)
    own_pos = (segment_order[:, None] * segment_rows + offsets_in).reshape(-1)
    all_totals, all_place = (
        lax.all_gather(segment_total, "seq", axis=0, tiled=True),
        lax.all_gather(segment_place, "seq", axis=0, tiled=True),
    )
    earlier = (all_place[None, :] < segment_place[:, None]).astype(jnp.float32)
    own_offset = jnp.sum(earlier * all_totals[None, :], axis=1)
    own_gate = (local_cum + own_offset[:, None]).reshape(-1)
    all_gate = lax.all_gather(own_gate, "seq", axis=0, tiled=True)
    all_pos = (all_place.astype(jnp.int32)[:, None] * segment_rows + offsets_in).reshape(-1)
    key_all, value_all = (
        lax.all_gather(keys, "seq", axis=0, tiled=True),
        lax.all_gather(values, "seq", axis=0, tiled=True),
    )
    block = 2048
    count = total_len // block

    def key_tile(block_index):
        start = block_index * block
        return (
            lax.dynamic_slice_in_dim(key_all, start, block),
            lax.dynamic_slice_in_dim(value_all, start, block),
            lax.dynamic_slice_in_dim(all_gate, start, block),
            lax.dynamic_slice_in_dim(all_pos, start, block),
        )

    def stats_step(block_index, carry):
        run_max, run_sum = carry
        key_rows, _, key_gate, key_pos = key_tile(block_index)
        scores, visible = tile_scores(
            queries, own_gate, own_pos, key_rows, key_gate, key_pos, score_scale
        )
        kept = jnp.where(visible, scores, masked_value)
        new_max = jnp.maximum(run_max, jnp.max(kept, axis=1))
        fresh = jnp.sum(jnp.where(visible, jnp.exp(kept - new_max[:, None]), 0.0), axis=1)
        return (new_max, run_sum * jnp.exp(run_max - new_max) + fresh)

    start_max = jnp.full((tokens_here,), masked_value, jnp.float32)
    run_max, run_sum = lax.fori_loop(
        0, count, stats_step, (start_max, jnp.zeros((tokens_here,), jnp.float32))
    )
    log_total = run_max + jnp.log(run_sum)

    def output_step(block_index, total):
        key_rows, value_rows, key_gate, key_pos = key_tile(block_index)
        scores, visible = tile_scores(
            queries, own_gate, own_pos, key_rows, key_gate, key_pos, score_scale
        )
        probs = tile_probs(scores, visible, log_total).astype(jnp.bfloat16)
        return total + jnp.dot(probs, value_rows, preferred_element_type=jnp.float32)

    out_full = lax.fori_loop(0, count, output_step, jnp.zeros((tokens_here, width), jnp.float32))
    attn_out = out_full.astype(jnp.bfloat16)
    row_delta = jnp.sum(out_grad.astype(jnp.float32) * out_full, axis=1)

    def row_terms(block_index):
        key_rows, value_rows, key_gate, key_pos = key_tile(block_index)
        scores, visible = tile_scores(
            queries, own_gate, own_pos, key_rows, key_gate, key_pos, score_scale
        )
        probs = tile_probs(scores, visible, log_total)
        dprob = contract_last(out_grad, value_rows)
        return (key_rows, probs, probs * (dprob - row_delta[:, None]))

    def query_step(block_index, total):
        key_rows, _, dscore = row_terms(block_index)
        return total + jnp.dot(
            dscore.astype(jnp.bfloat16), key_rows, preferred_element_type=jnp.float32
        )

    query_acc = lax.fori_loop(0, count, query_step, jnp.zeros((tokens_here, width), jnp.float32))
    query_all, grad_all = (
        lax.all_gather(queries, "seq", axis=0, tiled=True),
        lax.all_gather(out_grad, "seq", axis=0, tiled=True),
    )
    total_all, delta_all = (
        lax.all_gather(log_total, "seq", axis=0, tiled=True),
        lax.all_gather(row_delta, "seq", axis=0, tiled=True),
    )

    def column_step(block_index, carry):
        key_acc, value_acc, column_acc = carry
        start = block_index * block
        query_rows = lax.dynamic_slice_in_dim(query_all, start, block)
        grad_rows = lax.dynamic_slice_in_dim(grad_all, start, block)
        scores, visible = tile_scores(
            query_rows,
            lax.dynamic_slice_in_dim(all_gate, start, block),
            lax.dynamic_slice_in_dim(all_pos, start, block),
            keys,
            own_gate,
            own_pos,
            score_scale,
        )
        probs = tile_probs(scores, visible, lax.dynamic_slice_in_dim(total_all, start, block))
        dprob = contract_last(grad_rows, values)
        dscore = probs * (dprob - lax.dynamic_slice_in_dim(delta_all, start, block)[:, None])
        dscore_low = dscore.astype(jnp.bfloat16)
        key_acc = key_acc + contract_first(dscore_low, query_rows) * score_scale
        value_acc = value_acc + contract_first(probs.astype(jnp.bfloat16), grad_rows)
        column_acc = column_acc - jnp.sum(dscore, axis=0)
        return (key_acc, value_acc, column_acc)

    zeros_own = jnp.zeros((tokens_here, width), jnp.float32)
    key_grad, value_grad, gate_point = lax.fori_loop(
        0, count, column_step, (zeros_own, zeros_own, jnp.zeros((tokens_here,), jnp.float32))
    )
    query_grad = query_acc * score_scale
    point_rows = gate_point.reshape(2, segment_rows)
    within = jnp.flip(jnp.cumsum(jnp.flip(point_rows, 1), axis=1), 1)
    all_point = lax.all_gather(within[:, 0], "seq", axis=0, tiled=True)
    later = (all_place[None, :] > segment_place[:, None]).astype(jnp.float32)
    gate_grad = (within + jnp.sum(later * all_point[None, :], axis=1)[:, None]).reshape(-1)
    return (attn_out, query_grad, key_grad, value_grad, gate_grad)


LOG2E = 1.4426950408889634
META = 16


def pack_kernel(q_ref, k_ref, v_ref, g_ref, gate_hbm, order_hbm, out_ref, gate_ref, order_ref, sems):
    tokens = q_ref.shape[0]
    copies = [
        pltpu.make_async_copy(gate_hbm, gate_ref, sems.at[0]),
        pltpu.make_async_copy(order_hbm, order_ref, sems.at[1]),
    ]
    for index, ref in enumerate((q_ref, k_ref, v_ref, g_ref)):
        copies.append(
            pltpu.make_async_copy(
                ref, out_ref.at[pl.ds(index * tokens, tokens), :], sems.at[index + 2]
            )
        )
    for copy in copies:
        copy.start()
    copies[0].wait()
    copies[1].wait()
    gate = gate_ref[...]
    high = gate.astype(jnp.bfloat16).astype(jnp.float32)
    rest = gate - high
    mid = rest.astype(jnp.bfloat16).astype(jnp.float32)
    low = rest - mid
    lane = lax.broadcasted_iota(jnp.int32, (META, tokens), 1)
    row = lax.broadcasted_iota(jnp.int32, (META, tokens), 0)
    order = order_ref[...].astype(jnp.float32)
    place = jnp.where(lane < tokens // 2, order[:, 0:1], order[:, 1:2])
    meta = jnp.where(
        row == 0, high, jnp.where(row == 1, mid, jnp.where(row == 2, low, place))
    )
    out_ref[4 * tokens : 4 * tokens + META] = meta.astype(jnp.bfloat16)
    for copy in copies[2:]:
        copy.wait()


def split(items, turn, turns):
    return items[len(items) * turn // turns : len(items) * (turn + 1) // turns]


def block_order(steps):
    return list(range(steps))[::-1]


def sum_lanes(x, reverse):
    rows, lanes = x.shape
    pieces = []
    for _ in range(3):
        piece = x.astype(jnp.bfloat16)
        pieces.append(piece)
        x = x - piece.astype(jnp.float32)
    source = lax.broadcasted_iota(jnp.int32, (lanes, lanes), 0)
    target = lax.broadcasted_iota(jnp.int32, (lanes, lanes), 1)
    ones = (source >= target if reverse else source <= target).astype(jnp.float32)
    sums = jnp.dot(
        jnp.concatenate(pieces, axis=0),
        ones.astype(jnp.bfloat16),
        preferred_element_type=jnp.float32,
    )
    return (sums[2 * rows :] + sums[rows : 2 * rows]) + sums[:rows]


def roll_sum_rows(x, reverse):
    rows = x.shape[0]
    row = lax.broadcasted_iota(jnp.int32, x.shape, 0)
    step = 1
    while step < rows:
        if reverse:
            x = x + jnp.where(row < rows - step, pltpu.roll(x, rows - step, 0), 0.0)
        else:
            x = x + jnp.where(row >= step, pltpu.roll(x, step, 0), 0.0)
        step *= 2
    return x


def spread(column, width):
    return jnp.broadcast_to(column, (column.shape[0], width))


def halves(x, width):
    return [x[:, at : at + width] for at in range(0, x.shape[1], width)]


def log_total_of(pieces, width):
    best = pieces[0]
    for s in pieces[1:]:
        best = jnp.maximum(best, s)
    top = spread(jnp.max(best, axis=1, keepdims=True), width)
    mass = jnp.exp2(pieces[0] - top)
    for s in pieces[1:]:
        mass = mass + jnp.exp2(s - top)
    return top + spread(jnp.log2(jnp.sum(mass, axis=1, keepdims=True)), width)


def score_of(q, ks, key_row, tile, cols, factor):
    c0 = tile * cols
    return contract_last(q, ks[c0 : c0 + cols, :]) * factor - key_row[:, c0 : c0 + cols]


def start_rows(own, place, ks, key_row, own_s, own_total):
    total, width = ks.shape
    tokens = own_s.shape[0]
    seg = tokens // 2
    cols = 2 * tokens
    inner = lax.broadcasted_iota(jnp.int32, (tokens, 1), 0)
    row_pos = jnp.where(inner < seg, place[0] * seg + inner, place[1] * seg + inner - seg)
    q = own[0:tokens, :]
    pieces = []
    for tile in range(total // cols):
        c0 = tile * cols
        seen = lax.broadcasted_iota(jnp.int32, (tokens, cols), 1) + c0 <= row_pos
        s = score_of(q, ks, key_row, tile, cols, width ** (-0.5) * LOG2E)
        s = jnp.where(seen, s, masked_value)
        own_s[:, c0 : c0 + cols] = s
        pieces += halves(s, width)
    own_total[...] = log_total_of(pieces, width)


def row_kernel(own, ks, vs, own_s, own_total, out_ref, dq_ref):
    total, width = ks.shape
    tokens = out_ref.shape[0]
    cols = 2 * tokens
    g = own[3 * tokens : 4 * tokens, :]
    log_total = own_total[...]
    p, dps = [], []
    for tile in range(total // cols):
        c0 = tile * cols
        p += [jnp.exp2(s - log_total) for s in halves(own_s[:, c0 : c0 + cols], width)]
        dps += halves(contract_last(g, vs[c0 : c0 + cols, :]), width)
    low = jnp.concatenate([t.astype(jnp.bfloat16) for t in p], axis=1)
    out = jnp.dot(low, vs[...], preferred_element_type=jnp.float32)
    out_ref[...] = out.astype(jnp.bfloat16)
    delta = spread(jnp.sum(g.astype(jnp.float32) * out, axis=1, keepdims=True), width)
    low = jnp.concatenate(
        [(t * (dp - delta)).astype(jnp.bfloat16) for t, dp in zip(p, dps)], axis=1
    )
    dq_ref[...] = width ** (-0.5) * jnp.dot(low, ks[...], preferred_element_type=jnp.float32)


def core_kernel(counts, partner, tokens, width, core_ref, *refs):
    blocks = refs[: len(counts)]
    keep_ref, send_ref, ks, vs, own_s, own_total = refs[len(counts) : len(counts) + 6]
    qs, gs, cums, key_row, points, lines = refs[len(counts) + 6 :]
    seg = tokens // 2
    total = qs.shape[0]
    segments = total // seg
    size = 4 * tokens + META
    scale = width ** (-0.5)
    factor = scale * LOG2E
    lane1 = lax.broadcasted_iota(jnp.int32, (1, tokens), 1)
    left = lane1 < seg

    places = []
    for ref, count in zip(blocks, counts):
        for index in range(count):
            base = index * size
            meta = ref[base + 4 * tokens : base + size].astype(jnp.float32)
            gate = (meta[0:1] + meta[1:2]) + meta[2:3]
            place = meta[3:4].astype(jnp.int32)
            pair = (place[0, 0], place[0, seg])
            places.append((ref, base, pair))
            for half in range(2):
                at = pl.multiple_of(pair[half] * seg, seg)
                for slot, dest in enumerate((qs, ks)):
                    first = base + slot * tokens + half * seg
                    dest[pl.ds(at, seg), :] = ref[first : first + seg, :]
                shifted = gate if half == 0 else pltpu.roll(gate, seg, 1)
                cums[pl.ds(pair[half], 1), :] = jnp.where(left, shifted, 0.0)
    own_place = places[0][2]

    inside = sum_lanes(cums[...], False)
    whole = jnp.broadcast_to(inside[:, seg - 1 : seg], inside.shape)
    before = roll_sum_rows(whole, False) - whole
    cums[...] = (inside + before) * LOG2E
    for tile in range(segments // 2):
        even = cums[2 * tile : 2 * tile + 1, :]
        odd = pltpu.roll(cums[2 * tile + 1 : 2 * tile + 2, :], seg, 1)
        key_row[:, tile * tokens : (tile + 1) * tokens] = jnp.where(left, even, odd)

    for ref, base, pair in places:
        for half in range(2):
            at = pl.multiple_of(pair[half] * seg, seg)
            for slot, dest in ((2, vs), (3, gs)):
                first = base + slot * tokens + half * seg
                dest[pl.ds(at, seg), :] = ref[first : first + seg, :]

    points[...] = jnp.zeros_like(points)
    inner = lax.broadcasted_iota(jnp.int32, (tokens, 1), 0)
    own = blocks[0]

    other = blocks[partner]
    pair_k = jnp.concatenate([own[tokens : 2 * tokens, :], other[tokens : 2 * tokens, :]], axis=0)
    pair_v = jnp.concatenate(
        [own[2 * tokens : 3 * tokens, :], other[2 * tokens : 3 * tokens, :]], axis=0
    )
    firsts = [0, sum(counts[:partner])]
    pair_key, pair_pos = [], []
    for first in firsts:
        place = places[first][2]
        key = [cums[pl.ds(p, 1), :] for p in place]
        pair_key.append(jnp.where(left, key[0], pltpu.roll(key[1], seg, 1)))
        pair_pos.append(
            jnp.where(left, place[0] * seg + lane1, place[1] * seg + lane1 - seg)
        )
    pair_key = jnp.concatenate(pair_key, axis=1)
    pair_pos = jnp.concatenate(pair_pos, axis=1)

    rows, cols = tokens, 2 * tokens
    steps = total // cols
    core = core_ref[0, 0]
    row_in = lax.broadcasted_iota(jnp.int32, (rows, cols), 0) + core * rows
    col_in = lax.broadcasted_iota(jnp.int32, (rows, cols), 1)
    causal = col_in <= row_in
    state = {}

    def open_item(item):
        r0 = pl.multiple_of((2 * item + core) * rows, rows)
        state[item] = dict(
            q=qs[pl.ds(r0, rows), :], g=gs[pl.ds(r0, rows), :], r0=r0, tiles=item + 1,
            s=[], p=[], low=[],
        )

    def score_tile(item, tile):
        it = state[item]
        s = score_of(it["q"], ks, key_row, tile, cols, factor)
        if tile == item:
            s = jnp.where(causal, s, masked_value)
        it["s"] += halves(s, width)

    def prob_tile(item, tile):
        it = state[item]
        for s in it["s"][2 * tile : 2 * tile + 2]:
            p = jnp.exp2(s - it["total"])
            it["p"].append(p)
            it["low"].append(p.astype(jnp.bfloat16))

    def outputs(item):
        it = state[item]
        out = jnp.dot(
            jnp.concatenate(it["low"], axis=1),
            vs[: it["tiles"] * cols, :],
            preferred_element_type=jnp.float32,
        )
        g = it["g"].astype(jnp.float32)
        it["delta"] = spread(jnp.sum(g * out, axis=1, keepdims=True), width)

    sums = dict(k=jnp.zeros((cols, width), jnp.float32), v=jnp.zeros((cols, width), jnp.float32))

    def pair_columns(item):
        it = state[item]
        s = contract_last(it["q"], pair_k) * factor - pair_key
        seen = pair_pos <= it["r0"] + inner
        p = jnp.where(seen, jnp.exp2(s - jnp.concatenate([it["total"]] * 2, axis=1)), 0.0)
        ds = p * (contract_last(it["g"], pair_v) - jnp.concatenate([it["delta"]] * 2, axis=1))
        sums["v"] = sums["v"] + contract_first(p.astype(jnp.bfloat16), it["g"])
        sums["k"] = sums["k"] + contract_first(ds.astype(jnp.bfloat16), it["q"])

    def last_stage(item):
        it = state[item]
        for tile in range(it["tiles"]):
            c0 = tile * cols
            dp = halves(contract_last(it["g"], vs[c0 : c0 + cols, :]), width)
            for at in range(2):
                ds = it["p"][2 * tile + at] * (dp[at] - it["delta"])
                first = c0 + at * width
                points[:, first : first + width] += jnp.sum(
                    ds.reshape(rows // 8, 8, width), axis=0
                )
        pair_columns(item)

    order = block_order(steps)
    open_item(order[0])
    for tile in range(state[order[0]]["tiles"]):
        score_tile(order[0], tile)
    state[order[0]]["total"] = log_total_of(state[order[0]]["s"], width)
    start_rows(own, own_place, ks, key_row, own_s, own_total)
    for turn, item in enumerate(order):
        after = order[turn + 1] if turn + 1 < len(order) else None
        here = list(range(state[item]["tiles"]))
        ahead = []
        if after is not None:
            open_item(after)
            ahead = list(range(state[after]["tiles"]))
        count = max(len(here), len(ahead))
        for at in range(count):
            for tile in split(ahead, at, count):
                score_tile(after, tile)
            for tile in split(here, at, count):
                prob_tile(item, tile)
        outputs(item)
        if after is not None:
            state[after]["total"] = log_total_of(state[after]["s"], width)
        last_stage(item)

    for tile in range(total // width):
        lines[tile : tile + 1, :] = -jnp.sum(
            points[:, tile * width : (tile + 1) * width], axis=0, keepdims=True
        )
    inside = sum_lanes(lines[...], True)
    whole = jnp.broadcast_to(inside[:, 0:1], inside.shape)
    lines[...] = inside + (roll_sum_rows(whole, True) - whole)
    for index, ref in enumerate((keep_ref, send_ref)):
        ref[0:tokens, :] = sums["k"][index * tokens : (index + 1) * tokens, :] * scale
        ref[tokens : 2 * tokens, :] = sums["v"][index * tokens : (index + 1) * tokens, :]
        parts = []
        for half, place in enumerate(places[firsts[index]][2]):
            line = lines[pl.ds(place // 2, 1), :]
            parts.append(jnp.where(place % 2 == half, line, pltpu.roll(line, seg, 1)))
        ref[2 * tokens : 2 * tokens + 8, :] = jnp.broadcast_to(
            jnp.where(left, parts[0], parts[1]), (8, width)
        )


def join_kernel(keep_ref, got_ref, dk_ref, dv_ref, gate_ref):
    tokens = dk_ref.shape[0]
    dk_ref[...] = keep_ref[0:tokens, :] + got_ref[0:tokens, :]
    dv_ref[...] = keep_ref[tokens : 2 * tokens, :] + got_ref[tokens : 2 * tokens, :]
    gate_ref[...] = keep_ref[2 * tokens : 2 * tokens + 1, :] + got_ref[2 * tokens : 2 * tokens + 1, :]


def core_call(blocks, tokens, width, devices, core, partner):
    size = 4 * tokens + META
    counts = tuple(b.shape[0] // size for b in blocks)
    total = tokens * devices
    segments = 2 * devices
    vmem = pl.BlockSpec(memory_space=pltpu.VMEM)
    smem = pl.BlockSpec(memory_space=pltpu.SMEM)
    part = jax.ShapeDtypeStruct((2 * tokens + 8, width), jnp.float32)
    sorted_rows = jax.ShapeDtypeStruct((total, width), jnp.bfloat16)
    return pl.pallas_call(
        functools.partial(core_kernel, counts, partner, tokens, width),
        out_shape=(
            part,
            part,
            sorted_rows,
            sorted_rows,
            jax.ShapeDtypeStruct((tokens, total), jnp.float32),
            jax.ShapeDtypeStruct((tokens, width), jnp.float32),
        ),
        in_specs=[smem] + [vmem] * len(blocks),
        out_specs=[vmem] * 6,
        scratch_shapes=[
            pltpu.VMEM((total, width), jnp.bfloat16),
            pltpu.VMEM((total, width), jnp.bfloat16),
            pltpu.VMEM((segments, tokens), jnp.float32),
            pltpu.VMEM((1, total), jnp.float32),
            pltpu.VMEM((8, total), jnp.float32),
            pltpu.VMEM((total // width, width), jnp.float32),
        ],
        compiler_params=pltpu.CompilerParams(vmem_limit_bytes=40 * 2**20),
        name="core",
    )(core, *blocks)


def row_call(own, ks, vs, own_s, own_total, tokens, width):
    vmem = pl.BlockSpec(memory_space=pltpu.VMEM)
    return pl.pallas_call(
        row_kernel,
        out_shape=(
            jax.ShapeDtypeStruct((tokens, width), jnp.bfloat16),
            jax.ShapeDtypeStruct((tokens, width), jnp.float32),
        ),
        in_specs=[vmem] * 5,
        out_specs=[vmem] * 2,
        compiler_params=pltpu.CompilerParams(vmem_limit_bytes=24 * 2**20),
        cost_estimate=pl.CostEstimate(
            flops=6 * tokens * ks.shape[0] * width,
            bytes_accessed=4 * ks.shape[0] * width,
            transcendentals=tokens * ks.shape[0],
        ),
        name="rows",
    )(own, ks, vs, own_s, own_total)


def join_call(keep, got, tokens, width):
    vmem = pl.BlockSpec(memory_space=pltpu.VMEM)
    square = jax.ShapeDtypeStruct((tokens, width), jnp.float32)
    return pl.pallas_call(
        join_kernel,
        out_shape=(square, square, jax.ShapeDtypeStruct((1, width), jnp.float32)),
        in_specs=[vmem, vmem],
        out_specs=[vmem] * 3,
        compiler_params=pltpu.CompilerParams(vmem_limit_bytes=2 * 2**20),
        name="join",
    )(keep, got)


def shift(x, devices, ring=0, flip=0):
    line = devices // 4
    walk = [0] + list(range(1, line, 2)) + list(range(2, line, 2))[::-1]
    pairs = []
    for step, place in enumerate(walk):
        target = walk[(step + ring) % line]
        pairs += [(place * 4 + low, target * 4 + (low ^ flip)) for low in range(4)]
    return lax.ppermute(x, "seq", pairs)


MOVES = (
    ("down", "down", "own"),
    ("up", "up", "own"),
    ("own_core", "core", "own"),
    ("side", "side", "own"),
    ("down_down", "down", "down"),
    ("down_side", "side", "down"),
    ("side_up", "up", "side"),
    ("up_core", "core", "up"),
    ("last", "side", "down_down"),
    ("down_core", "core", "down"),
    ("down_side_core", "core", "down_side"),
    ("side_core", "core", "side"),
    ("side_up_core", "core", "side_up"),
    ("down_down_core", "core", "down_down"),
    ("last_core", "core", "last"),
)
KINDS = {"up": {"ring": 1}, "down": {"ring": -1}, "side": {"flip": 2}, "core": {"flip": 1}}


def gather_blocks(x, devices):
    blocks = {"own": x}
    for name, kind, sent in MOVES:
        blocks[name] = shift(blocks[sent], devices, **KINDS[kind])
    return list(blocks.values())


def local_small(queries, keys, values, log_gate, out_grad, segment_order):
    tokens, width = queries.shape
    devices = lax.axis_size("seq")
    vmem = pl.BlockSpec(memory_space=pltpu.VMEM)
    packed = pl.pallas_call(
        pack_kernel,
        out_shape=jax.ShapeDtypeStruct((4 * tokens + META, width), jnp.bfloat16),
        in_specs=[pl.BlockSpec(memory_space=pltpu.HBM)] * 6,
        out_specs=vmem,
        scratch_shapes=[
            pltpu.VMEM((1, tokens), jnp.float32),
            pltpu.VMEM((1, 2), jnp.int32),
            pltpu.SemaphoreType.DMA((6,)),
        ],
        compiler_params=pltpu.CompilerParams(vmem_limit_bytes=2 * 2**20),
        name="pack",
    )(*[pltpu.with_memory_space_constraint(t, pltpu.HBM) for t in (queries, keys, values, out_grad, log_gate.reshape(1, tokens), segment_order.reshape(1, 2))])
    blocks = gather_blocks(packed, devices)
    core = (lax.axis_index("seq") % 2).astype(jnp.int32).reshape(1, 1)
    partner = 1 + [m[0] for m in MOVES].index("own_core")
    keep, send, ks, vs, own_s, own_total = core_call(blocks, tokens, width, devices, core, partner)
    got = shift(send, devices, flip=1)
    out, dq = row_call(packed, ks, vs, own_s, own_total, tokens, width)
    dk, dv, gate = join_call(keep, got, tokens, width)
    return (out, dq, dk, dv, gate.reshape(tokens))


def local(queries, keys, values, log_gate, out_grad, segment_order):
    tokens, width = queries.shape
    small = tokens == width and lax.axis_size("seq") == len(MOVES) + 1
    path = local_small if small else local_general
    return path(queries, keys, values, log_gate, out_grad, segment_order)


def solution(mesh):
    placed = (
        P(("grp", "seq"), None),
        P(("grp", "seq"), None),
        P(("grp", "seq"), None),
        P(("grp", "seq")),
        P(("grp", "seq"), None),
        P(("grp", "seq")),
    )
    return jax.shard_map(
        local,
        mesh=mesh,
        in_specs=placed,
        out_specs=(
            P(("grp", "seq"), None),
            P(("grp", "seq"), None),
            P(("grp", "seq"), None),
            P(("grp", "seq"), None),
            P(("grp", "seq")),
        ),
        check_vma=False,
    )
```

```python
import functools

import jax
import jax.numpy as jnp
from jax import lax
from jax.experimental import pallas as pl
from jax.experimental.pallas import tpu as pltpu
from jax.sharding import PartitionSpec as P


masked_value = -1e30


def contract_last(left, right):
    return lax.dot_general(
        left, right, (((1,), (1,)), ((), ())), preferred_element_type=jnp.float32
    )


def contract_first(left, right):
    return lax.dot_general(
        left, right, (((0,), (0,)), ((), ())), preferred_element_type=jnp.float32
    )


def tile_scores(query_rows, query_gate, query_pos, key_rows, key_gate, key_pos, score_scale):
    scores = (
        contract_last(query_rows, key_rows) * score_scale + query_gate[:, None] - key_gate[None, :]
    )
    visible = key_pos[None, :] <= query_pos[:, None]
    return (scores, visible)


def tile_probs(scores, visible, row_total):
    return jnp.where(visible, jnp.exp(scores - row_total[:, None]), 0.0)


def local_general(queries, keys, values, log_gate, out_grad, segment_order):
    tokens_here, width = queries.shape
    devices = lax.axis_size("seq")
    segment_rows = tokens_here // 2
    total_len = tokens_here * devices
    score_scale = width ** (-0.5)
    offsets_in = lax.broadcasted_iota(jnp.int32, (1, segment_rows), 1)
    local_cum = jnp.cumsum(log_gate.reshape(2, segment_rows), axis=1)
    segment_total = local_cum[:, -1]
    segment_place = segment_order.astype(jnp.float32)
    own_pos = (segment_order[:, None] * segment_rows + offsets_in).reshape(-1)
    all_totals, all_place = (
        lax.all_gather(segment_total, "seq", axis=0, tiled=True),
        lax.all_gather(segment_place, "seq", axis=0, tiled=True),
    )
    earlier = (all_place[None, :] < segment_place[:, None]).astype(jnp.float32)
    own_offset = jnp.sum(earlier * all_totals[None, :], axis=1)
    own_gate = (local_cum + own_offset[:, None]).reshape(-1)
    all_gate = lax.all_gather(own_gate, "seq", axis=0, tiled=True)
    all_pos = (all_place.astype(jnp.int32)[:, None] * segment_rows + offsets_in).reshape(-1)
    key_all, value_all = (
        lax.all_gather(keys, "seq", axis=0, tiled=True),
        lax.all_gather(values, "seq", axis=0, tiled=True),
    )
    block = 2048
    count = total_len // block

    def key_tile(block_index):
        start = block_index * block
        return (
            lax.dynamic_slice_in_dim(key_all, start, block),
            lax.dynamic_slice_in_dim(value_all, start, block),
            lax.dynamic_slice_in_dim(all_gate, start, block),
            lax.dynamic_slice_in_dim(all_pos, start, block),
        )

    def stats_step(block_index, carry):
        run_max, run_sum = carry
        key_rows, _, key_gate, key_pos = key_tile(block_index)
        scores, visible = tile_scores(
            queries, own_gate, own_pos, key_rows, key_gate, key_pos, score_scale
        )
        kept = jnp.where(visible, scores, masked_value)
        new_max = jnp.maximum(run_max, jnp.max(kept, axis=1))
        fresh = jnp.sum(jnp.where(visible, jnp.exp(kept - new_max[:, None]), 0.0), axis=1)
        return (new_max, run_sum * jnp.exp(run_max - new_max) + fresh)

    start_max = jnp.full((tokens_here,), masked_value, jnp.float32)
    run_max, run_sum = lax.fori_loop(
        0, count, stats_step, (start_max, jnp.zeros((tokens_here,), jnp.float32))
    )
    log_total = run_max + jnp.log(run_sum)

    def output_step(block_index, total):
        key_rows, value_rows, key_gate, key_pos = key_tile(block_index)
        scores, visible = tile_scores(
            queries, own_gate, own_pos, key_rows, key_gate, key_pos, score_scale
        )
        probs = tile_probs(scores, visible, log_total).astype(jnp.bfloat16)
        return total + jnp.dot(probs, value_rows, preferred_element_type=jnp.float32)

    out_full = lax.fori_loop(0, count, output_step, jnp.zeros((tokens_here, width), jnp.float32))
    attn_out = out_full.astype(jnp.bfloat16)
    row_delta = jnp.sum(out_grad.astype(jnp.float32) * out_full, axis=1)

    def row_terms(block_index):
        key_rows, value_rows, key_gate, key_pos = key_tile(block_index)
        scores, visible = tile_scores(
            queries, own_gate, own_pos, key_rows, key_gate, key_pos, score_scale
        )
        probs = tile_probs(scores, visible, log_total)
        dprob = contract_last(out_grad, value_rows)
        return (key_rows, probs, probs * (dprob - row_delta[:, None]))

    def query_step(block_index, total):
        key_rows, _, dscore = row_terms(block_index)
        return total + jnp.dot(
            dscore.astype(jnp.bfloat16), key_rows, preferred_element_type=jnp.float32
        )

    query_acc = lax.fori_loop(0, count, query_step, jnp.zeros((tokens_here, width), jnp.float32))
    query_all, grad_all = (
        lax.all_gather(queries, "seq", axis=0, tiled=True),
        lax.all_gather(out_grad, "seq", axis=0, tiled=True),
    )
    total_all, delta_all = (
        lax.all_gather(log_total, "seq", axis=0, tiled=True),
        lax.all_gather(row_delta, "seq", axis=0, tiled=True),
    )

    def column_step(block_index, carry):
        key_acc, value_acc, column_acc = carry
        start = block_index * block
        query_rows = lax.dynamic_slice_in_dim(query_all, start, block)
        grad_rows = lax.dynamic_slice_in_dim(grad_all, start, block)
        scores, visible = tile_scores(
            query_rows,
            lax.dynamic_slice_in_dim(all_gate, start, block),
            lax.dynamic_slice_in_dim(all_pos, start, block),
            keys,
            own_gate,
            own_pos,
            score_scale,
        )
        probs = tile_probs(scores, visible, lax.dynamic_slice_in_dim(total_all, start, block))
        dprob = contract_last(grad_rows, values)
        dscore = probs * (dprob - lax.dynamic_slice_in_dim(delta_all, start, block)[:, None])
        dscore_low = dscore.astype(jnp.bfloat16)
        key_acc = key_acc + contract_first(dscore_low, query_rows) * score_scale
        value_acc = value_acc + contract_first(probs.astype(jnp.bfloat16), grad_rows)
        column_acc = column_acc - jnp.sum(dscore, axis=0)
        return (key_acc, value_acc, column_acc)

    zeros_own = jnp.zeros((tokens_here, width), jnp.float32)
    key_grad, value_grad, gate_point = lax.fori_loop(
        0, count, column_step, (zeros_own, zeros_own, jnp.zeros((tokens_here,), jnp.float32))
    )
    query_grad = query_acc * score_scale
    point_rows = gate_point.reshape(2, segment_rows)
    within = jnp.flip(jnp.cumsum(jnp.flip(point_rows, 1), axis=1), 1)
    all_point = lax.all_gather(within[:, 0], "seq", axis=0, tiled=True)
    later = (all_place[None, :] > segment_place[:, None]).astype(jnp.float32)
    gate_grad = (within + jnp.sum(later * all_point[None, :], axis=1)[:, None]).reshape(-1)
    return (attn_out, query_grad, key_grad, value_grad, gate_grad)


LOG2E = 1.4426950408889634
META = 16


def pack_kernel(q_ref, k_ref, v_ref, g_ref, gate_hbm, order_hbm, out_ref, gate_ref, order_ref, sems):
    tokens = q_ref.shape[0]
    copies = [
        pltpu.make_async_copy(gate_hbm, gate_ref, sems.at[0]),
        pltpu.make_async_copy(order_hbm, order_ref, sems.at[1]),
    ]
    for index, ref in enumerate((q_ref, k_ref, v_ref, g_ref)):
        copies.append(
            pltpu.make_async_copy(
                ref, out_ref.at[pl.ds(index * tokens, tokens), :], sems.at[index + 2]
            )
        )
    for copy in copies:
        copy.start()
    copies[0].wait()
    copies[1].wait()
    gate = gate_ref[...]
    high = gate.astype(jnp.bfloat16).astype(jnp.float32)
    rest = gate - high
    mid = rest.astype(jnp.bfloat16).astype(jnp.float32)
    low = rest - mid
    lane = lax.broadcasted_iota(jnp.int32, (META, tokens), 1)
    row = lax.broadcasted_iota(jnp.int32, (META, tokens), 0)
    order = order_ref[...].astype(jnp.float32)
    place = jnp.where(lane < tokens // 2, order[:, 0:1], order[:, 1:2])
    meta = jnp.where(
        row == 0, high, jnp.where(row == 1, mid, jnp.where(row == 2, low, place))
    )
    out_ref[4 * tokens : 4 * tokens + META] = meta.astype(jnp.bfloat16)
    for copy in copies[2:]:
        copy.wait()


def split(items, turn, turns):
    return items[len(items) * turn // turns : len(items) * (turn + 1) // turns]


def block_order(steps):
    return list(range(steps))[::-1]


def sum_lanes(x, reverse):
    rows, lanes = x.shape
    pieces = []
    for _ in range(3):
        piece = x.astype(jnp.bfloat16)
        pieces.append(piece)
        x = x - piece.astype(jnp.float32)
    source = lax.broadcasted_iota(jnp.int32, (lanes, lanes), 0)
    target = lax.broadcasted_iota(jnp.int32, (lanes, lanes), 1)
    ones = (source >= target if reverse else source <= target).astype(jnp.float32)
    sums = jnp.dot(
        jnp.concatenate(pieces, axis=0),
        ones.astype(jnp.bfloat16),
        preferred_element_type=jnp.float32,
    )
    return (sums[2 * rows :] + sums[rows : 2 * rows]) + sums[:rows]


def roll_sum_rows(x, reverse):
    rows = x.shape[0]
    row = lax.broadcasted_iota(jnp.int32, x.shape, 0)
    step = 1
    while step < rows:
        if reverse:
            x = x + jnp.where(row < rows - step, pltpu.roll(x, rows - step, 0), 0.0)
        else:
            x = x + jnp.where(row >= step, pltpu.roll(x, step, 0), 0.0)
        step *= 2
    return x


def spread(column, width):
    return jnp.broadcast_to(column, (column.shape[0], width))


def halves(x, width):
    return [x[:, at : at + width] for at in range(0, x.shape[1], width)]


def log_total_of(pieces, width):
    best = pieces[0]
    for s in pieces[1:]:
        best = jnp.maximum(best, s)
    top = spread(jnp.max(best, axis=1, keepdims=True), width)
    mass = jnp.exp2(pieces[0] - top)
    for s in pieces[1:]:
        mass = mass + jnp.exp2(s - top)
    return top + spread(jnp.log2(jnp.sum(mass, axis=1, keepdims=True)), width)


def score_of(q, ks, key_row, tile, cols, factor):
    c0 = tile * cols
    return contract_last(q, ks[c0 : c0 + cols, :]) * factor - key_row[:, c0 : c0 + cols]


def start_rows(own, place, ks, key_row, own_s, own_total):
    total, width = ks.shape
    tokens = own_s.shape[0]
    seg = tokens // 2
    cols = 2 * tokens
    inner = lax.broadcasted_iota(jnp.int32, (tokens, 1), 0)
    row_pos = jnp.where(inner < seg, place[0] * seg + inner, place[1] * seg + inner - seg)
    q = own[0:tokens, :]
    pieces = []
    for tile in range(total // cols):
        c0 = tile * cols
        seen = lax.broadcasted_iota(jnp.int32, (tokens, cols), 1) + c0 <= row_pos
        s = score_of(q, ks, key_row, tile, cols, width ** (-0.5) * LOG2E)
        s = jnp.where(seen, s, masked_value)
        own_s[:, c0 : c0 + cols] = s
        pieces += halves(s, width)
    own_total[...] = log_total_of(pieces, width)


def row_kernel(own, ks, vs, own_s, own_total, out_ref, dq_ref):
    total, width = ks.shape
    tokens = out_ref.shape[0]
    cols = 2 * tokens
    g = own[3 * tokens : 4 * tokens, :]
    log_total = own_total[...]
    p, dps = [], []
    for tile in range(total // cols):
        c0 = tile * cols
        p += [jnp.exp2(s - log_total) for s in halves(own_s[:, c0 : c0 + cols], width)]
        dps += halves(contract_last(g, vs[c0 : c0 + cols, :]), width)
    low = jnp.concatenate([t.astype(jnp.bfloat16) for t in p], axis=1)
    out = jnp.dot(low, vs[...], preferred_element_type=jnp.float32)
    out_ref[...] = out.astype(jnp.bfloat16)
    delta = spread(jnp.sum(g.astype(jnp.float32) * out, axis=1, keepdims=True), width)
    low = jnp.concatenate(
        [(t * (dp - delta)).astype(jnp.bfloat16) for t, dp in zip(p, dps)], axis=1
    )
    dq_ref[...] = width ** (-0.5) * jnp.dot(low, ks[...], preferred_element_type=jnp.float32)


def core_kernel(counts, partner, tokens, width, core_ref, *refs):
    blocks = refs[: len(counts)]
    keep_ref, send_ref, ks, vs, own_s, own_total = refs[len(counts) : len(counts) + 6]
    qs, gs, cums, key_row, points, lines = refs[len(counts) + 6 :]
    seg = tokens // 2
    total = qs.shape[0]
    segments = total // seg
    size = 4 * tokens + META
    scale = width ** (-0.5)
    factor = scale * LOG2E
    lane1 = lax.broadcasted_iota(jnp.int32, (1, tokens), 1)
    left = lane1 < seg

    places = []
    for ref, count in zip(blocks, counts):
        for index in range(count):
            base = index * size
            meta = ref[base + 4 * tokens : base + size].astype(jnp.float32)
            gate = (meta[0:1] + meta[1:2]) + meta[2:3]
            place = meta[3:4].astype(jnp.int32)
            pair = (place[0, 0], place[0, seg])
            places.append((ref, base, pair))
            for half in range(2):
                at = pl.multiple_of(pair[half] * seg, seg)
                for slot, dest in enumerate((qs, ks)):
                    first = base + slot * tokens + half * seg
                    dest[pl.ds(at, seg), :] = ref[first : first + seg, :]
                shifted = gate if half == 0 else pltpu.roll(gate, seg, 1)
                cums[pl.ds(pair[half], 1), :] = jnp.where(left, shifted, 0.0)
    own_place = places[0][2]

    inside = sum_lanes(cums[...], False)
    whole = jnp.broadcast_to(inside[:, seg - 1 : seg], inside.shape)
    before = roll_sum_rows(whole, False) - whole
    cums[...] = (inside + before) * LOG2E
    for tile in range(segments // 2):
        even = cums[2 * tile : 2 * tile + 1, :]
        odd = pltpu.roll(cums[2 * tile + 1 : 2 * tile + 2, :], seg, 1)
        key_row[:, tile * tokens : (tile + 1) * tokens] = jnp.where(left, even, odd)

    for ref, base, pair in places:
        for half in range(2):
            at = pl.multiple_of(pair[half] * seg, seg)
            for slot, dest in ((2, vs), (3, gs)):
                first = base + slot * tokens + half * seg
                dest[pl.ds(at, seg), :] = ref[first : first + seg, :]

    points[...] = jnp.zeros_like(points)
    inner = lax.broadcasted_iota(jnp.int32, (tokens, 1), 0)
    own = blocks[0]

    other = blocks[partner]
    pair_k = jnp.concatenate([own[tokens : 2 * tokens, :], other[tokens : 2 * tokens, :]], axis=0)
    pair_v = jnp.concatenate(
        [own[2 * tokens : 3 * tokens, :], other[2 * tokens : 3 * tokens, :]], axis=0
    )
    firsts = [0, sum(counts[:partner])]
    pair_key, pair_pos = [], []
    for first in firsts:
        place = places[first][2]
        key = [cums[pl.ds(p, 1), :] for p in place]
        pair_key.append(jnp.where(left, key[0], pltpu.roll(key[1], seg, 1)))
        pair_pos.append(
            jnp.where(left, place[0] * seg + lane1, place[1] * seg + lane1 - seg)
        )
    pair_key = jnp.concatenate(pair_key, axis=1)
    pair_pos = jnp.concatenate(pair_pos, axis=1)

    rows, cols = tokens, 2 * tokens
    steps = total // cols
    core = core_ref[0, 0]
    row_in = lax.broadcasted_iota(jnp.int32, (rows, cols), 0) + core * rows
    col_in = lax.broadcasted_iota(jnp.int32, (rows, cols), 1)
    causal = col_in <= row_in
    state = {}

    def open_item(item):
        r0 = pl.multiple_of((2 * item + core) * rows, rows)
        state[item] = dict(
            q=qs[pl.ds(r0, rows), :], g=gs[pl.ds(r0, rows), :], r0=r0, tiles=item + 1,
            s=[], p=[], low=[],
        )

    def score_tile(item, tile):
        it = state[item]
        s = score_of(it["q"], ks, key_row, tile, cols, factor)
        if tile == item:
            s = jnp.where(causal, s, masked_value)
        it["s"] += halves(s, width)

    def prob_tile(item, tile):
        it = state[item]
        for s in it["s"][2 * tile : 2 * tile + 2]:
            p = jnp.exp2(s - it["total"])
            it["p"].append(p)
            it["low"].append(p.astype(jnp.bfloat16))

    def outputs(item):
        it = state[item]
        out = jnp.dot(
            jnp.concatenate(it["low"], axis=1),
            vs[: it["tiles"] * cols, :],
            preferred_element_type=jnp.float32,
        )
        g = it["g"].astype(jnp.float32)
        it["delta"] = spread(jnp.sum(g * out, axis=1, keepdims=True), width)

    sums = dict(k=jnp.zeros((cols, width), jnp.float32), v=jnp.zeros((cols, width), jnp.float32))

    def pair_columns(item):
        it = state[item]
        s = contract_last(it["q"], pair_k) * factor - pair_key
        seen = pair_pos <= it["r0"] + inner
        p = jnp.where(seen, jnp.exp2(s - jnp.concatenate([it["total"]] * 2, axis=1)), 0.0)
        ds = p * (contract_last(it["g"], pair_v) - jnp.concatenate([it["delta"]] * 2, axis=1))
        sums["v"] = sums["v"] + contract_first(p.astype(jnp.bfloat16), it["g"])
        sums["k"] = sums["k"] + contract_first(ds.astype(jnp.bfloat16), it["q"])

    def last_stage(item):
        it = state[item]
        for tile in range(it["tiles"]):
            c0 = tile * cols
            dp = halves(contract_last(it["g"], vs[c0 : c0 + cols, :]), width)
            for at in range(2):
                ds = it["p"][2 * tile + at] * (dp[at] - it["delta"])
                first = c0 + at * width
                points[:, first : first + width] += jnp.sum(
                    ds.reshape(rows // 8, 8, width), axis=0
                )
        pair_columns(item)

    order = block_order(steps)
    open_item(order[0])
    for tile in range(state[order[0]]["tiles"]):
        score_tile(order[0], tile)
    state[order[0]]["total"] = log_total_of(state[order[0]]["s"], width)
    start_rows(own, own_place, ks, key_row, own_s, own_total)
    for turn, item in enumerate(order):
        after = order[turn + 1] if turn + 1 < len(order) else None
        here = list(range(state[item]["tiles"]))
        ahead = []
        if after is not None:
            open_item(after)
            ahead = list(range(state[after]["tiles"]))
        count = max(len(here), len(ahead))
        for at in range(count):
            for tile in split(ahead, at, count):
                score_tile(after, tile)
            for tile in split(here, at, count):
                prob_tile(item, tile)
        outputs(item)
        if after is not None:
            state[after]["total"] = log_total_of(state[after]["s"], width)
        last_stage(item)

    for tile in range(total // width):
        lines[tile : tile + 1, :] = -jnp.sum(
            points[:, tile * width : (tile + 1) * width], axis=0, keepdims=True
        )
    inside = sum_lanes(lines[...], True)
    whole = jnp.broadcast_to(inside[:, 0:1], inside.shape)
    lines[...] = inside + (roll_sum_rows(whole, True) - whole)
    for index, ref in enumerate((keep_ref, send_ref)):
        ref[0:tokens, :] = sums["k"][index * tokens : (index + 1) * tokens, :] * scale
        ref[tokens : 2 * tokens, :] = sums["v"][index * tokens : (index + 1) * tokens, :]
        parts = []
        for half, place in enumerate(places[firsts[index]][2]):
            line = lines[pl.ds(place // 2, 1), :]
            parts.append(jnp.where(place % 2 == half, line, pltpu.roll(line, seg, 1)))
        ref[2 * tokens : 2 * tokens + 8, :] = jnp.broadcast_to(
            jnp.where(left, parts[0], parts[1]), (8, width)
        )


def join_kernel(keep_ref, got_ref, rows_out, rows_dq, dk_ref, dv_ref, gate_ref, out_ref, dq_ref):
    tokens = dk_ref.shape[0]
    out_ref[...] = rows_out[...]
    dq_ref[...] = rows_dq[...]
    dk_ref[...] = keep_ref[0:tokens, :] + got_ref[0:tokens, :]
    dv_ref[...] = keep_ref[tokens : 2 * tokens, :] + got_ref[tokens : 2 * tokens, :]
    gate_ref[...] = keep_ref[2 * tokens : 2 * tokens + 1, :] + got_ref[2 * tokens : 2 * tokens + 1, :]


def core_call(blocks, tokens, width, devices, core, partner):
    size = 4 * tokens + META
    counts = tuple(b.shape[0] // size for b in blocks)
    total = tokens * devices
    segments = 2 * devices
    vmem = pl.BlockSpec(memory_space=pltpu.VMEM)
    smem = pl.BlockSpec(memory_space=pltpu.SMEM)
    part = jax.ShapeDtypeStruct((2 * tokens + 8, width), jnp.float32)
    sorted_rows = jax.ShapeDtypeStruct((total, width), jnp.bfloat16)
    return pl.pallas_call(
        functools.partial(core_kernel, counts, partner, tokens, width),
        out_shape=(
            part,
            part,
            sorted_rows,
            sorted_rows,
            jax.ShapeDtypeStruct((tokens, total), jnp.float32),
            jax.ShapeDtypeStruct((tokens, width), jnp.float32),
        ),
        in_specs=[smem] + [vmem] * len(blocks),
        out_specs=[vmem] * 6,
        scratch_shapes=[
            pltpu.VMEM((total, width), jnp.bfloat16),
            pltpu.VMEM((total, width), jnp.bfloat16),
            pltpu.VMEM((segments, tokens), jnp.float32),
            pltpu.VMEM((1, total), jnp.float32),
            pltpu.VMEM((8, total), jnp.float32),
            pltpu.VMEM((total // width, width), jnp.float32),
        ],
        compiler_params=pltpu.CompilerParams(vmem_limit_bytes=40 * 2**20),
        name="core",
    )(core, *blocks)


def row_call(own, ks, vs, own_s, own_total, tokens, width):
    vmem = pl.BlockSpec(memory_space=pltpu.VMEM)
    return pl.pallas_call(
        row_kernel,
        out_shape=(
            jax.ShapeDtypeStruct((tokens, width), jnp.bfloat16),
            jax.ShapeDtypeStruct((tokens, width), jnp.float32),
        ),
        in_specs=[vmem] * 5,
        out_specs=[vmem] * 2,
        compiler_params=pltpu.CompilerParams(vmem_limit_bytes=24 * 2**20),
        cost_estimate=pl.CostEstimate(
            flops=6 * tokens * ks.shape[0] * width,
            bytes_accessed=4 * ks.shape[0] * width,
            transcendentals=tokens * ks.shape[0],
        ),
        name="rows",
    )(own, ks, vs, own_s, own_total)


def join_call(keep, got, out, dq, tokens, width):
    vmem = pl.BlockSpec(memory_space=pltpu.VMEM)
    square = jax.ShapeDtypeStruct((tokens, width), jnp.float32)
    return pl.pallas_call(
        join_kernel,
        out_shape=(
            square,
            square,
            jax.ShapeDtypeStruct((1, width), jnp.float32),
            jax.ShapeDtypeStruct((tokens, width), jnp.bfloat16),
            square,
        ),
        in_specs=[vmem] * 4,
        out_specs=[vmem] * 5,
        compiler_params=pltpu.CompilerParams(vmem_limit_bytes=2 * 2**20),
        name="join",
    )(keep, got, out, dq)


def shift(x, devices, ring=0, flip=0):
    line = devices // 4
    walk = [0] + list(range(1, line, 2)) + list(range(2, line, 2))[::-1]
    pairs = []
    for step, place in enumerate(walk):
        target = walk[(step + ring) % line]
        pairs += [(place * 4 + low, target * 4 + (low ^ flip)) for low in range(4)]
    return lax.ppermute(x, "seq", pairs)


MOVES = (
    ("down", "down", "own"),
    ("up", "up", "own"),
    ("own_core", "core", "own"),
    ("side", "side", "own"),
    ("down_down", "down", "down"),
    ("down_side", "side", "down"),
    ("side_up", "up", "side"),
    ("up_core", "core", "up"),
    ("last", "side", "down_down"),
    ("down_core", "core", "down"),
    ("down_side_core", "core", "down_side"),
    ("side_core", "core", "side"),
    ("side_up_core", "core", "side_up"),
    ("down_down_core", "core", "down_down"),
    ("last_core", "core", "last"),
)
KINDS = {"up": {"ring": 1}, "down": {"ring": -1}, "side": {"flip": 2}, "core": {"flip": 1}}


def gather_blocks(x, devices):
    blocks = {"own": x}
    for name, kind, sent in MOVES:
        blocks[name] = shift(blocks[sent], devices, **KINDS[kind])
    return list(blocks.values())


def local_small(queries, keys, values, log_gate, out_grad, segment_order):
    tokens, width = queries.shape
    devices = lax.axis_size("seq")
    vmem = pl.BlockSpec(memory_space=pltpu.VMEM)
    packed = pl.pallas_call(
        pack_kernel,
        out_shape=jax.ShapeDtypeStruct((4 * tokens + META, width), jnp.bfloat16),
        in_specs=[pl.BlockSpec(memory_space=pltpu.HBM)] * 6,
        out_specs=vmem,
        scratch_shapes=[
            pltpu.VMEM((1, tokens), jnp.float32),
            pltpu.VMEM((1, 2), jnp.int32),
            pltpu.SemaphoreType.DMA((6,)),
        ],
        compiler_params=pltpu.CompilerParams(vmem_limit_bytes=2 * 2**20),
        name="pack",
    )(*[pltpu.with_memory_space_constraint(t, pltpu.HBM) for t in (queries, keys, values, out_grad, log_gate.reshape(1, tokens), segment_order.reshape(1, 2))])
    blocks = gather_blocks(packed, devices)
    core = (lax.axis_index("seq") % 2).astype(jnp.int32).reshape(1, 1)
    partner = 1 + [m[0] for m in MOVES].index("own_core")
    keep, send, ks, vs, own_s, own_total = core_call(blocks, tokens, width, devices, core, partner)
    got = shift(send, devices, flip=1)
    out, dq = row_call(packed, ks, vs, own_s, own_total, tokens, width)
    dk, dv, gate, out, dq = join_call(keep, got, out, dq, tokens, width)
    return (out, dq, dk, dv, gate.reshape(tokens))


def local(queries, keys, values, log_gate, out_grad, segment_order):
    tokens, width = queries.shape
    small = tokens == width and lax.axis_size("seq") == len(MOVES) + 1
    path = local_small if small else local_general
    return path(queries, keys, values, log_gate, out_grad, segment_order)


def solution(mesh):
    placed = (
        P(("grp", "seq"), None),
        P(("grp", "seq"), None),
        P(("grp", "seq"), None),
        P(("grp", "seq")),
        P(("grp", "seq"), None),
        P(("grp", "seq")),
    )
    return jax.shard_map(
        local,
        mesh=mesh,
        in_specs=placed,
        out_specs=(
            P(("grp", "seq"), None),
            P(("grp", "seq"), None),
            P(("grp", "seq"), None),
            P(("grp", "seq"), None),
            P(("grp", "seq")),
        ),
        check_vma=False,
    )
```
